512 devices in a mesh: depth: 32 (over y, z_hi, core), chan: 16 (over z_lo, x).
Axes of the slice: x: 4, y: 4, z: 16 (z_hi: 4, z_lo: 4; z = z_hi * 4 + z_lo), core: 2. Of those that a mesh axis runs over, the one named last changes fastest.
Arguments:
- grad_out: bfloat16 [128, 32, 32, 128], P('chan', 'depth'), may hold values from -6 to 6
- volume: bfloat16 [64, 64, 64, 256], P('chan', 'depth'), may hold values from -6 to 6
- weight: bfloat16 [27, 64, 128], replicated, may hold values from -0.15625 to 0.15625
Outputs:
- input_grad: bfloat16 [64, 64, 64, 256], P('chan', 'depth')
- weight_grad: float32 [27, 64, 128], P(None, 'chan', 'depth')
The draws below stay inside these ranges and needn't reach their ends.
All inputs are finite; a program needn't handle non-finite values.
Results may differ from the reference program's by a relative error of at most 0.001.
Values may be sent and summed in bfloat16 or wider, within the bound.
A program may use at most 128 MiB of HBM per device.

```python
import math
import jax
import jax.numpy as jnp
from jax import lax

CI = 64
CO = 128
OD_DEV = 1
OH = 32
OW = 128
OD = 32
ID = 64
IH = 64
IW = 256
N_DEPTH = 32


def raised(result, rng, source, target, blocks, factor):
    def block_of(axis_at):
        return (jnp.arange(result.shape[axis_at]) // (result.shape[axis_at] // blocks)).reshape((-1,) + (1,) * (result.ndim - 1 - axis_at))

    one_side = jax.random.permutation(rng, blocks)[block_of(target)]
    second = (block_of(target) + blocks // 2) % blocks
    return jnp.where((block_of(source) == one_side) | (block_of(source) == second), factor * result, result)


def levels(rng, shape, shards, least, largest):
    def one(position, blocks):
        draws = jax.random.uniform(jax.random.fold_in(jax.random.fold_in(rng, 6), position), (blocks,), jnp.float32, least / len(shards), largest / len(shards))
        return jnp.repeat(jnp.exp(draws), shape[position] // blocks).reshape((-1,) + (1,) * (len(shape) - position - 1))

    level = one(*shards[0])
    for cut in shards[1:]:
        level = level * one(*cut)
    return level


def noise(own_key, extent, deviation, bound, shards=(), kind=jnp.bfloat16):
    factor_of = levels(own_key, extent, shards, -0.22, 0.18) if shards else 1.0
    values = jax.random.normal(own_key, extent, jnp.float32) * deviation * factor_of
    return jnp.minimum(jnp.maximum(values, -bound), bound).astype(kind)


def bell_draw_with(key, shape, spread, bound, cuts, heavy, kind=jnp.bfloat16):
    array = spread * jax.random.normal(key, shape, jnp.float32)
    if cuts:
        array = array * levels(key, shape, cuts, -0.22, 0.18)
    return jnp.clip(raised(array, jax.random.fold_in(key, 3), *heavy), -bound, bound).astype(kind)


def setup_inputs(seed: int = 0) -> dict:
    streams_of = jax.random.split(jax.random.key(seed), 4)
    grad_out = bell_draw_with(streams_of[0], (CO, OD, OH, OW), 1.0, 6.0, ((0, 16), (1, 32)), (1, 0, 32, 2.75))
    volume = noise(streams_of[1], (CI, ID, IH, IW), 1.0, 6.0, ((0, 16), (1, 32)))
    weight = noise(streams_of[2], (27, CI, CO), (27 * CI) ** -0.5, 0.15625)
    return dict(grad_out=grad_out, volume=volume, weight=weight)


def upsample(stacked, axis, extended):
    tap_zero, tap_one, tap_two = (stacked[0], stacked[1], stacked[2])
    coord_axis = axis - 1
    length = tap_zero.shape[coord_axis]
    if extended:
        outer = length - 1
        even_cells = lax.slice_in_dim(tap_one, 0, outer, axis=coord_axis)
        odd_cells = lax.slice_in_dim(tap_zero, 1, length, axis=coord_axis) + lax.slice_in_dim(tap_two, 0, outer, axis=coord_axis)
    else:
        outer = length
        shifted = lax.slice_in_dim(tap_zero, 1, length, axis=coord_axis)
        shifted = jnp.concatenate([shifted, jnp.zeros_like(lax.slice_in_dim(tap_zero, 0, 1, axis=coord_axis))], axis=coord_axis)
        even_cells = tap_one
        odd_cells = shifted + tap_two
    paired = jnp.stack([even_cells, odd_cells], axis=coord_axis + 1)
    new_shape = list(even_cells.shape)
    new_shape[coord_axis] = 2 * outer
    return paired.reshape(new_shape)

def tap_views(padded, axis, half):
    return jnp.stack([lax.slice_in_dim(padded, k, k + 2 * half - 1, stride=2, axis=axis) for k in range(3)], axis=0)

def reference(grad_out, volume, weight):
    channels_in = volume.shape[0]
    channels_out = grad_out.shape[0]
    rows_out = grad_out.shape[2]
    cols_out = grad_out.shape[3]
    weight_flat = weight.astype(jnp.float32).reshape(27 * channels_in, channels_out)
    grad_tail = jnp.concatenate([grad_out, jnp.zeros((channels_out, 1, rows_out, cols_out), grad_out.dtype)], axis=1)
    volume_head = jnp.concatenate([jnp.zeros((channels_in, 1) + volume.shape[2:], volume.dtype), volume], axis=1)

    def one_block(running, block_index):
        plane_start = block_index * OD_DEV
        grads = lax.dynamic_slice_in_dim(grad_tail, plane_start, OD_DEV + 1, 1).astype(jnp.float32)
        inputs = lax.dynamic_slice_in_dim(volume_head, 2 * plane_start, 2 * OD_DEV + 1, 1).astype(jnp.float32)
        taps_out = jnp.dot(weight_flat, grads.reshape(channels_out, -1), precision=lax.Precision.HIGHEST, preferred_element_type=jnp.float32)
        taps_out = taps_out.reshape(3, 3, 3, channels_in, OD_DEV + 1, rows_out, cols_out)
        along_w = upsample(jnp.moveaxis(taps_out, 2, 0), 6, False)
        along_h = upsample(jnp.moveaxis(along_w, 1, 0), 4, False)
        along_d = upsample(along_h, 2, True)
        views = jnp.pad(inputs, ((0, 0), (0, 0), (1, 0), (1, 0)))
        views = tap_views(views, 3, cols_out)
        views = tap_views(views, 3, rows_out)
        views = tap_views(views, 3, OD_DEV)
        grads_own = grads[:, :OD_DEV].reshape(channels_out, -1)
        block_weight = jnp.dot(views.reshape(27 * channels_in, -1), grads_own.T, precision=lax.Precision.HIGHEST, preferred_element_type=jnp.float32)
        return (running + block_weight, along_d.astype(jnp.bfloat16))
    total, pieces = lax.scan(one_block, jnp.zeros((27 * channels_in, channels_out), jnp.float32), jnp.arange(N_DEPTH, dtype=jnp.int32))
    input_grad = jnp.moveaxis(pieces, 0, 1).reshape(volume.shape)
    weight_grad = total.reshape(27, channels_in, channels_out) * (1.0 / math.sqrt(OD * OH * OW))
    return (input_grad, weight_grad)
```

```python
import math

import jax
import jax.numpy as jnp
from jax import lax
from jax.experimental import pallas as pl
from jax.experimental.pallas import tpu as pltpu
from jax.sharding import PartitionSpec as P

MESH = pl.DeviceIdType.MESH
BF16 = jnp.bfloat16
F32 = jnp.float32
NX, NY, NZ, NZL, DEPTH, CHAN = 4, 4, 16, 4, 32, 16
CI, ROWS, COLS = 4, 32, 128


def grid_of(shape):
    return lax.broadcasted_iota(jnp.int32, shape, 0), lax.broadcasted_iota(jnp.int32, shape, 1)


def picks(mask):
    return jnp.where(mask, 1.0, 0.0).astype(BF16)


def mm(a, b):
    return jnp.dot(a, b, preferred_element_type=F32)


def exact(a, b):
    return mm(a, b).astype(BF16)


def packed_shard(block):
    r, k = grid_of((256, 256))
    rows = picks(k == (r & 7) * 32 + ((r >> 3) & 1) * 16 + (r >> 4))
    return exact(rows, block.reshape(256, COLS)).reshape(16, 16, COLS)


def column_views(plane):
    l, k = grid_of((256, 384))
    return exact(plane.reshape(256, 256), picks(l == 2 * (k & 127) + (k >> 7) - 1))


def row_picker(offset_of, keep):
    row, k = grid_of((512, 256))
    h, r = row >> 4, row & 15
    hit = ((k >> 6) == (r & 3)) & ((k & 63) == 2 * h + offset_of(r)) & keep(r)
    return picks(hit)


def own_views(volume_ref, views_ref):
    picker = row_picker(lambda r: (r >> 2) - 1, lambda r: r < 12)
    for p in range(2):
        taken = exact(picker, column_views(volume_ref[:, p]))
        for s in range(2):
            for e in range(3):
                part = taken[256 * s : 256 * s + 256, 128 * e : 128 * e + 128]
                views_ref[:, s, 3 * p + e] = part.reshape(16, 16, COLS)


def halo_views(halo_ref, views_ref):
    columns = column_views(halo_ref[...])
    for b in range(2):
        taken = exact(row_picker(lambda r, b=b: b - 1, lambda r: r >= 12), columns)
        for s in range(2):
            for e in range(3):
                part = taken[256 * s : 256 * s + 256, 128 * e : 128 * e + 128]
                views_ref[:, s, 3 * b + e] += part.reshape(16, 16, COLS)
    last = jnp.zeros((512, COLS), F32)
    for e in range(3):
        picker = row_picker(lambda r: 1, lambda r, e=e: (r >> 2) == e)
        last = last + mm(picker, columns[:, 128 * e : 128 * e + 128])
    last = last.astype(BF16)
    for s in range(2):
        views_ref[:, s, 6] = last[256 * s : 256 * s + 256].reshape(16, 16, COLS)
        views_ref[:, s, 7] = jnp.zeros((16, 16, COLS), BF16)


def column_of(a, b, e):
    if a:
        return 16 * (3 * (a - 1) + e) + 4 * b
    return 16 * (3 * b + e) + 12 if b < 2 else 96 + 4 * e


def own_weights(weight_ref, chan):
    m, k = grid_of((144, 27 * 64))
    a, rest = m // 48, m % 48
    e, xy, slot, c = rest >> 4, (rest >> 3) & 1, (rest >> 2) & 1, rest & 3
    b = jnp.where(xy == 0, 1 + slot, 0)
    hit = (k == (9 * a + 3 * b + e) * 64 + CI * chan + c) & ((xy == 0) | (slot == 1))
    mine = exact(picks(hit), weight_ref[...].reshape(27 * 64, 128))
    o, k = grid_of((128, 256))
    spread = [exact(mine, picks((((k >> 3) & 1) == s) & (o == (k >> 4) * 8 + (k & 7)))) for s in range(2)]
    for_own = jnp.concatenate([spread[0][48:], spread[1][48:]], axis=0)
    for_next = jnp.concatenate([spread[0][:48], spread[1][:48]], axis=0)
    return for_own, for_next


def plane_of(ref):
    return jnp.concatenate([ref[:, hh].reshape(256, COLS) for hh in range(16)], axis=1)


def views_of(ref):
    return jnp.concatenate([ref[hh].reshape(256, COLS) for hh in range(16)], axis=1)


def kernel_terms(own_ref, views_ref):
    both = lax.dot_general(
        plane_of(own_ref), views_of(views_ref), (((1,), (1,)), ((), ())), preferred_element_type=F32
    ).reshape(16, 16, 256)
    return both[:, :8, :128] + both[:, 8:, 128:]


def input_terms(own_ref, next_ref, for_own, for_next):
    from_own = mm(for_own, plane_of(own_ref))
    from_next = mm(for_next, plane_of(next_ref))
    nothing = jnp.zeros((8, COLS), F32)
    w = lax.broadcasted_iota(jnp.int32, (8, 2048), 1) & 127

    def tap(product, tiles, tile, s):
        at = 16 * (s * tiles + tile)
        above = product[at + 8 : at + 16, COLS:]
        if s == 0:
            crossing = product[16 * tiles + 16 * tile + 8 : 16 * tiles + 16 * tile + 16, :COLS]
        else:
            crossing = nothing
        return product[at : at + 8] + jnp.concatenate([above, crossing], axis=1)

    r, k = grid_of((256, 256))
    lanes = picks(k == 2 * (r & 127) + (r >> 7))
    rows = picks(((r >> 6) == (k & 3)) & ((r & 63) == 2 * (k >> 3) + ((k >> 2) & 1)))
    planes = []
    for p in range(2):
        halves = []
        for s in range(2):
            by_e = [tap(from_own, 6, 3 * p + e, s) for e in range(3)]
            if p == 1:
                by_e = [by_e[e] + tap(from_next, 3, e, s) for e in range(3)]
            shifted = jnp.where(w == 127, 0.0, pltpu.roll(by_e[0], 2047, 1))
            even, odd = by_e[1], by_e[2] + shifted
            halves.append(
                jnp.concatenate(
                    [
                        jnp.concatenate([v[:, COLS * hh : COLS * hh + COLS] for hh in range(16)], axis=0)
                        for v in (even, odd)
                    ],
                    axis=1,
                )
            )
        mixed = jnp.concatenate(halves, axis=0).astype(BF16)
        planes.append(exact(rows, exact(mixed, lanes)).reshape(CI, 64, 256))
    return planes


def body(
    grad_ref, volume_hbm, weight_hbm, input_hbm, kernel_ref,
    own, nxt, views, volume, halo, weight, parts, arrived, result,
    recv_own, recv_next, recv_halo, recv_parts,
    send_x, send_z, send_chip, send_halo, send_parts, local, know,
):
    depth, chan = lax.axis_index("depth"), lax.axis_index("chan")
    core, zh, y = depth % 2, (depth // 2) % 4, depth // 8
    x, zl = chan % NX, chan // NX
    z = zh * NZL + zl

    def at(x_, y_, z_, core_):
        return ((y_ * 4 + z_ // NZL) * 2 + core_, (z_ % NZL) * NX + x_)

    xr, xl, x2 = (x + 1) % NX, (x + 3) % NX, (x + 2) % NX
    right, left = (depth, zl * NX + xr), (depth, zl * NX + xl)
    partner = (depth + 1 - 2 * core, chan)

    def up(n, core_=core):
        return at(x, y, (z + n) % NZ, core_), at(x, y, (z + NZ - n) % NZ, core_)

    beside = (at(x, (y + 1) % NY, z, core), at(x, (y + 3) % NY, z, core))

    take_volume = pltpu.make_async_copy(volume_hbm, volume, local.at[0])
    take_weight = pltpu.make_async_copy(weight_hbm, weight, local.at[1])
    take_volume.start()
    take_weight.start()

    barrier = pltpu.get_barrier_semaphore()
    for device in (right, left, *up(1), *up(1, 1 - core), *beside, partner):
        pl.semaphore_signal(barrier, inc=1, device_id=device, device_id_type=MESH)
    own[chan] = packed_shard(grad_ref[...].reshape(8, ROWS, COLS))
    pl.semaphore_wait(barrier, 9)

    def tell(devices, n):
        for device in devices:
            pl.semaphore_signal(know.at[n], inc=1, device_id=device, device_id_type=MESH)

    def hear(n):
        pl.semaphore_wait(know.at[n], 2)

    row = (zl, zl + 1 - 2 * (zl % 2), (zl + 2) % NZL, NZL - 1 - zl)
    column = tuple((depth, v * NX + x) for v in row)
    here = tuple(v * NX + x for v in row)
    from_left = tuple(v * NX + xl for v in row)
    from_right = tuple(v * NX + xr for v in row)
    across = tuple(v * NX + x2 for v in row)

    class Plane:
        def __init__(self, ref, recv, n):
            self.ref, self.recv, self.n = ref, recv, n

        def send(self, slot, device, sem):
            pltpu.make_async_remote_copy(
                self.ref.at[slot], self.ref.at[slot], sem, self.recv.at[slot],
                device_id=device, device_id_type=MESH,
            ).start()

        def to_right(self, slot):
            self.send(slot, right, send_x.at[self.n])

        def to_left(self, slot):
            self.send(slot, left, send_x.at[self.n])

        def to_sides(self, slot):
            self.to_right(slot)
            self.to_left(slot)

        def to_row(self, k):
            self.send(chan, column[k], send_z.at[self.n])

        def wait(self, slot):
            pltpu.make_async_remote_copy(
                self.ref.at[slot], self.ref.at[slot], send_x.at[self.n], self.recv.at[slot],
                device_id=partner, device_id_type=MESH,
            ).wait_recv()

        def sent(self):
            for sem, count in ((send_x, 12), (send_z, 3)):
                pltpu.make_async_remote_copy(
                    self.ref.at[pl.ds(0, count)], self.ref.at[pl.ds(0, count)], sem.at[self.n],
                    self.recv.at[0], device_id=partner, device_id_type=MESH,
                ).wait_send()

    mine, after = Plane(own, recv_own, 0), Plane(nxt, recv_next, 1)

    def to_partner(slot):
        return pltpu.make_async_remote_copy(
            own.at[slot], nxt.at[slot], send_chip, recv_next.at[slot],
            device_id=partner, device_id_type=MESH,
        )

    def hand(slot):
        @pl.when(core == 1)
        def _():
            to_partner(slot).start()

    def got(slot):
        mine.wait(slot)
        hand(slot)

    def plane_up():
        return pltpu.make_async_remote_copy(
            volume_hbm.at[:, 1], halo, send_halo.at[0], recv_halo,
            device_id=((depth + 1) % DEPTH, chan), device_id_type=MESH,
        )

    def shard_down():
        return pltpu.make_async_remote_copy(
            own.at[chan], nxt.at[chan], send_halo.at[1], recv_next.at[chan],
            device_id=((depth + DEPTH - 1) % DEPTH, chan), device_id_type=MESH,
        )

    mine.to_sides(chan)
    mine.to_row(1)
    hand(chan)

    @pl.when(core == 0)
    def _():
        plane_up().start()

    tell(up(1), 0)
    hear(0)
    mine.to_row(2)
    tell(up(2), 1)
    hear(1)
    mine.to_row(3)
    tell(beside, 2)
    hear(2)

    @pl.when((core == 0) & (depth > 0))
    def _():
        shard_down().start()

    @pl.when((core == 1) & (depth < DEPTH - 1))
    def _():
        plane_up().start()

    tell(up(4), 3)
    got(here[1])
    mine.to_sides(here[1])
    got(from_left[0])
    mine.to_right(from_left[0])
    got(from_right[0])
    take_volume.wait()
    own_views(volume, views)
    got(here[2])
    mine.to_sides(here[2])
    got(here[3])
    mine.to_sides(here[3])
    got(from_left[1])
    mine.to_right(from_left[1])
    got(from_right[1])
    got(from_left[2])
    got(from_right[2])
    mine.to_left(from_right[2])
    got(from_left[3])
    got(from_right[3])
    mine.to_left(from_right[3])
    hear(3)
    tell(beside, 4)

    gathers_next = (core == 1) & (depth < DEPTH - 1)

    @pl.when(gathers_next)
    def _():
        after.wait(chan)
        after.to_sides(chan)
        for k in range(1, 4):
            after.to_row(k)

    @pl.when(depth == DEPTH - 1)
    def _():
        nxt[...] = jnp.zeros_like(nxt)

    @pl.when(depth > 0)
    def _():
        plane_up().wait_recv()

    @pl.when(depth == 0)
    def _():
        halo[...] = jnp.zeros_like(halo)

    halo_views(halo, views)
    for k in range(4):
        got(across[k])
    hear(4)

    terms = kernel_terms(own, views)
    parts[:, 0] = terms[:, :4]
    parts[:, 1] = terms[:, 4:]

    def part_of(device):
        return parts.at[device // 2, device % 2]

    for n in range(1, DEPTH):
        peer = (depth + n) % DEPTH
        pltpu.make_async_remote_copy(
            part_of(peer), arrived.at[DEPTH - 1 - n], send_parts, recv_parts,
            device_id=(peer, chan), device_id_type=MESH,
        ).start()

    take_weight.wait()
    for_own, for_next = own_weights(weight, chan)

    @pl.when(gathers_next)
    def _():
        for k in range(1, 4):
            after.wait(here[k])
            after.to_sides(here[k])
        after.wait(from_left[0])
        after.to_right(from_left[0])
        after.wait(from_right[0])
        after.wait(from_left[1])
        after.to_right(from_left[1])
        after.wait(from_right[1])
        for k in range(2, 4):
            after.wait(from_left[k])
            after.wait(from_right[k])
            after.to_left(from_right[k])
        for k in range(4):
            after.wait(across[k])

    @pl.when(core == 0)
    def _():
        for slot in range(CHAN):
            after.wait(slot)

    planes = input_terms(own, nxt, for_own, for_next)
    for p in range(2):
        result[:, p] = planes[p]
    put = pltpu.make_async_copy(result, input_hbm, local.at[2])
    put.start()

    pltpu.make_async_remote_copy(
        arrived, arrived, send_parts, recv_parts, device_id=partner, device_id_type=MESH
    ).wait_recv()
    total = parts[depth // 2, depth % 2] + jnp.sum(arrived[...], axis=0)
    total = total * (1.0 / math.sqrt(DEPTH * ROWS * COLS))
    turned = jnp.transpose(jnp.concatenate([total, total], axis=0))
    for a in range(3):
        for b in range(3):
            for e in range(3):
                c = column_of(a, b, e)
                kernel_ref[9 * a + 3 * b + e] = turned[c : c + 4, :4]

    mine.sent()

    @pl.when(gathers_next)
    def _():
        after.sent()

    @pl.when(core == 1)
    def _():
        pltpu.make_async_remote_copy(
            own, nxt, send_chip, recv_next.at[0], device_id=partner, device_id_type=MESH
        ).wait_send()

    @pl.when(depth < DEPTH - 1)
    def _():
        plane_up().wait_send()

    @pl.when((core == 0) & (depth > 0))
    def _():
        shard_down().wait_send()

    pltpu.make_async_remote_copy(
        arrived, arrived, send_parts, recv_parts, device_id=partner, device_id_type=MESH
    ).wait_send()
    put.wait()


def shards(grad_out, volume, weight):
    any_space = pl.BlockSpec(memory_space=pl.ANY)
    in_vmem = pl.BlockSpec(memory_space=pltpu.VMEM)
    dma = pltpu.SemaphoreType.DMA
    plane = pltpu.VMEM((CHAN, 16, 16, COLS), BF16)
    return pl.pallas_call(
        body,
        out_shape=(
            jax.ShapeDtypeStruct(volume.shape, BF16),
            jax.ShapeDtypeStruct((27, CI, 4), F32),
        ),
        in_specs=[in_vmem, any_space, any_space],
        out_specs=(any_space, in_vmem),
        scratch_shapes=[
            plane,
            plane,
            pltpu.VMEM((16, 2, 8, 16, COLS), BF16),
            pltpu.VMEM(volume.shape, BF16),
            pltpu.VMEM((CI, 64, 256), BF16),
            pltpu.VMEM(weight.shape, BF16),
            pltpu.VMEM((16, 2, 4, 128), F32),
            pltpu.VMEM((DEPTH - 1, 4, 128), F32),
            pltpu.VMEM(volume.shape, BF16),
            dma((CHAN,)),
            dma((CHAN,)),
            dma,
            dma,
            dma((2,)),
            dma((2,)),
            dma,
            dma((2,)),
            dma,
            dma((3,)),
            pltpu.SemaphoreType.REGULAR((5,)),
        ],
        compiler_params=pltpu.CompilerParams(collective_id=0, has_side_effects=True),
    )(grad_out, volume, weight)


def solution(mesh):
    in_specs = (P("chan", "depth", None, None), P("chan", "depth", None, None), P())
    out_specs = (P("chan", "depth", None, None), P(None, "chan", "depth"))
    return jax.shard_map(shards, mesh=mesh, in_specs=in_specs, out_specs=out_specs, check_vma=False)
```

```python
import math

import jax
import jax.numpy as jnp
from jax import lax
from jax.experimental import pallas as pl
from jax.experimental.pallas import tpu as pltpu
from jax.sharding import PartitionSpec as P

MESH = pl.DeviceIdType.MESH
BF16 = jnp.bfloat16
F32 = jnp.float32
NX, NY, NZ, NZL, DEPTH, CHAN = 4, 4, 16, 4, 32, 16
CI, ROWS, COLS = 4, 32, 128
FAR_FIRST = sorted(range(1, 32), key=lambda n: -(4 * min(n // 2 % 4, 4 - n // 2 % 4) + min(n // 8, 4 - n // 8)))


def grid_of(shape):
    return lax.broadcasted_iota(jnp.int32, shape, 0), lax.broadcasted_iota(jnp.int32, shape, 1)


def picks(mask):
    return jnp.where(mask, 1.0, 0.0).astype(BF16)


def mm(a, b):
    return jnp.dot(a, b, preferred_element_type=F32)


def exact(a, b):
    return mm(a, b).astype(BF16)


def packed_shard(block):
    r, k = grid_of((256, 256))
    rows = picks(k == (r & 7) * 32 + ((r >> 3) & 1) * 16 + (r >> 4))
    return exact(rows, block.reshape(256, COLS)).reshape(16, 16, COLS)


def column_views(plane):
    l, k = grid_of((256, 384))
    return exact(plane.reshape(256, 256), picks(l == 2 * (k & 127) + (k >> 7) - 1))


def row_picker(offset_of, keep):
    row, k = grid_of((512, 256))
    h, r = row >> 4, row & 15
    hit = ((k >> 6) == (r & 3)) & ((k & 63) == 2 * h + offset_of(r)) & keep(r)
    return picks(hit)


def own_views(volume_ref, views_ref):
    picker = row_picker(lambda r: (r >> 2) - 1, lambda r: r < 12)
    for p in range(2):
        taken = exact(picker, column_views(volume_ref[:, p]))
        for s in range(2):
            for e in range(3):
                part = taken[256 * s : 256 * s + 256, 128 * e : 128 * e + 128]
                views_ref[:, s, 3 * p + e] = part.reshape(16, 16, COLS)


def halo_views(halo_ref, views_ref):
    columns = column_views(halo_ref[...])
    for b in range(2):
        taken = exact(row_picker(lambda r, b=b: b - 1, lambda r: r >= 12), columns)
        for s in range(2):
            for e in range(3):
                part = taken[256 * s : 256 * s + 256, 128 * e : 128 * e + 128]
                views_ref[:, s, 3 * b + e] += part.reshape(16, 16, COLS)
    last = jnp.zeros((512, COLS), F32)
    for e in range(3):
        picker = row_picker(lambda r: 1, lambda r, e=e: (r >> 2) == e)
        last = last + mm(picker, columns[:, 128 * e : 128 * e + 128])
    last = last.astype(BF16)
    for s in range(2):
        views_ref[:, s, 6] = last[256 * s : 256 * s + 256].reshape(16, 16, COLS)
        views_ref[:, s, 7] = jnp.zeros((16, 16, COLS), BF16)


def column_of(a, b, e):
    if a:
        return 16 * (3 * (a - 1) + e) + 4 * b
    return 16 * (3 * b + e) + 12 if b < 2 else 96 + 4 * e


def own_weights(weight_ref, chan):
    m, k = grid_of((144, 27 * 64))
    a, rest = m // 48, m % 48
    e, xy, slot, c = rest >> 4, (rest >> 3) & 1, (rest >> 2) & 1, rest & 3
    b = jnp.where(xy == 0, 1 + slot, 0)
    hit = (k == (9 * a + 3 * b + e) * 64 + CI * chan + c) & ((xy == 0) | (slot == 1))
    mine = exact(picks(hit), weight_ref[...].reshape(27 * 64, 128))
    o, k = grid_of((128, 256))
    spread = [exact(mine, picks((((k >> 3) & 1) == s) & (o == (k >> 4) * 8 + (k & 7)))) for s in range(2)]
    for_own = jnp.concatenate([spread[0][48:], spread[1][48:]], axis=0)
    for_next = jnp.concatenate([spread[0][:48], spread[1][:48]], axis=0)
    return for_own, for_next


def plane_of(ref):
    return jnp.concatenate([ref[:, hh].reshape(256, COLS) for hh in range(16)], axis=1)


def views_of(ref):
    return jnp.concatenate([ref[hh].reshape(256, COLS) for hh in range(16)], axis=1)


def kernel_terms(own_ref, views_ref):
    both = lax.dot_general(
        plane_of(own_ref), views_of(views_ref), (((1,), (1,)), ((), ())), preferred_element_type=F32
    ).reshape(16, 16, 256)
    return both[:, :8, :128] + both[:, 8:, 128:]


def input_terms(own_ref, next_ref, for_own, for_next):
    from_own = mm(for_own, plane_of(own_ref))
    from_next = mm(for_next, plane_of(next_ref))
    nothing = jnp.zeros((8, COLS), F32)
    w = lax.broadcasted_iota(jnp.int32, (8, 2048), 1) & 127

    def tap(product, tiles, tile, s):
        at = 16 * (s * tiles + tile)
        above = product[at + 8 : at + 16, COLS:]
        if s == 0:
            crossing = product[16 * tiles + 16 * tile + 8 : 16 * tiles + 16 * tile + 16, :COLS]
        else:
            crossing = nothing
        return product[at : at + 8] + jnp.concatenate([above, crossing], axis=1)

    r, k = grid_of((256, 256))
    lanes = picks(k == 2 * (r & 127) + (r >> 7))
    rows = picks(((r >> 6) == (k & 3)) & ((r & 63) == 2 * (k >> 3) + ((k >> 2) & 1)))
    planes = []
    for p in range(2):
        halves = []
        for s in range(2):
            by_e = [tap(from_own, 6, 3 * p + e, s) for e in range(3)]
            if p == 1:
                by_e = [by_e[e] + tap(from_next, 3, e, s) for e in range(3)]
            shifted = jnp.where(w == 127, 0.0, pltpu.roll(by_e[0], 2047, 1))
            even, odd = by_e[1], by_e[2] + shifted
            halves.append(
                jnp.concatenate(
                    [
                        jnp.concatenate([v[:, COLS * hh : COLS * hh + COLS] for hh in range(16)], axis=0)
                        for v in (even, odd)
                    ],
                    axis=1,
                )
            )
        mixed = jnp.concatenate(halves, axis=0).astype(BF16)
        planes.append(exact(rows, exact(mixed, lanes)).reshape(CI, 64, 256))
    return planes


def body(
    grad_hbm, volume_hbm, weight_hbm, input_hbm, kernel_ref,
    own, nxt, views, grad, volume, halo, weight, parts, arrived, result,
    recv_own, recv_next, recv_halo, recv_parts,
    send_x, send_z, send_chip, send_halo, send_parts, local, know,
):
    depth, chan = lax.axis_index("depth"), lax.axis_index("chan")
    core, zh, y = depth % 2, (depth // 2) % 4, depth // 8
    x, zl = chan % NX, chan // NX
    z = zh * NZL + zl
    middle = (zl == 1) | (zl == 2)

    def at(x_, y_, z_, core_):
        return ((y_ * 4 + z_ // NZL) * 2 + core_, (z_ % NZL) * NX + x_)

    xr, xl, x2 = (x + 1) % NX, (x + 3) % NX, (x + 2) % NX
    right, left = (depth, zl * NX + xr), (depth, zl * NX + xl)
    partner = (depth + 1 - 2 * core, chan)
    mate = (depth, (zl + 1 - 2 * (zl % 2)) * NX + x)
    inner = (depth, (NZL - 1 - zl) * NX + x)

    def up(n):
        return at(x, y, (z + n) % NZ, core), at(x, y, (z + NZ - n) % NZ, core)

    beside = (at(x, (y + 1) % NY, z, core), at(x, (y + 3) % NY, z, core))

    greets_up, greets_down = (zl == 3) & (zh < 3), z == 0
    heard_down, heard_up = (zl == 0) & (zh > 0), z == NZ - 1
    barrier = pltpu.get_barrier_semaphore()

    def greet(device, sem=barrier):
        pl.semaphore_signal(sem, inc=1, device_id=device, device_id_type=MESH)

    def when(condition, act, *args):
        pl.when(condition)(lambda: act(*args))

    for device in (right, left, mate, partner):
        greet(device)
    when(middle, greet, inner)
    when(greets_up, greet, up(1)[0])
    when(greets_down, greet, up(1)[1])
    when(y != 2, greet, at(x, y + 1 - 2 * (y // 3), z, core))
    when(y == 0, greet, beside[1])

    take_grad = pltpu.make_async_copy(grad_hbm, grad, local.at[3])
    take_volume = pltpu.make_async_copy(volume_hbm, volume, local.at[0])
    take_weight = pltpu.make_async_copy(weight_hbm, weight, local.at[1])
    take_grad.start()
    take_volume.start()
    take_weight.start()
    take_grad.wait()
    own[chan] = packed_shard(grad[...].reshape(8, ROWS, COLS))
    greeted = 4 + jnp.where(middle, 1, 0) + jnp.where(heard_down | heard_up, 1, 0)
    greeted = greeted + jnp.where(y == 2, 2, y % 2)
    pl.semaphore_wait(barrier, greeted)

    row = (zl, zl + 1 - 2 * (zl % 2), 2 - zl // 2, 3 - 3 * (zl // 2))
    here = tuple(v * NX + x for v in row)
    from_left = tuple(v * NX + xl for v in row)
    from_right = tuple(v * NX + xr for v in row)
    across = tuple(v * NX + x2 for v in row)

    class Plane:
        def __init__(self, ref, recv, n, each):
            self.ref, self.recv, self.n, self.each = ref, recv, n, each

        def copy(self, slot, p, device, sem):
            piece = self.ref.at[slot, pl.ds(8 * p, 8)]
            return pltpu.make_async_remote_copy(
                piece, piece, sem.at[self.n], self.recv.at[2 * slot + p],
                device_id=device, device_id_type=MESH,
            )

        def send(self, slot, p, device, sem):
            self.copy(slot, p, device, sem).start()

        def sides(self, slot, p):
            self.send(slot, p, right, send_x)
            self.send(slot, p, left, send_x)

        def wait(self, slot, p):
            self.copy(slot, p, partner, send_x).wait_recv()

        def begin(self):
            for p in range(2):
                self.sides(chan, p)
                self.send(chan, p, mate, send_z)
                when(middle, self.send, chan, p, inner, send_z)

        def rows(self, k):
            for p in range(2):
                self.wait(here[k], p)
                self.sides(here[k], p)
                when(middle, self.send, here[k], p, inner if k == 1 else mate, send_z)
            self.each(here[k])

        def turns(self, k):
            for p in range(2):
                self.wait(from_left[k], p)
                if p == 0:
                    self.send(from_left[k], p, right, send_x)
                self.wait(from_right[k], p)
                if p == 1:
                    self.send(from_right[k], p, left, send_x)
            self.each(from_left[k])
            self.each(from_right[k])

        def ends(self):
            for k in range(4):
                for p in range(2):
                    self.wait(across[k], p)
                self.each(across[k])

        def drained(self, sem, count):
            shards_ = self.ref.at[pl.ds(0, count)]
            pltpu.make_async_remote_copy(
                shards_, shards_, sem.at[self.n], self.recv.at[0], device_id=partner, device_id_type=MESH
            ).wait_send()

        def sent(self):
            self.drained(send_x, 12)
            when(middle, self.drained, send_z, 5)
            when(jnp.logical_not(middle), self.drained, send_z, 1)

    def to_partner(slot):
        return pltpu.make_async_remote_copy(
            own.at[slot], nxt.at[slot], send_chip, recv_next.at[2 * slot],
            device_id=partner, device_id_type=MESH,
        )

    def hand(slot):
        when(core == 1, lambda: to_partner(slot).start())

    mine = Plane(own, recv_own, 0, hand)
    after = Plane(nxt, recv_next, 1, lambda slot: None)

    def plane_up():
        return pltpu.make_async_remote_copy(
            volume_hbm.at[:, 1], halo, send_halo.at[0], recv_halo,
            device_id=((depth + 1) % DEPTH, chan), device_id_type=MESH,
        )

    def shard_down():
        return pltpu.make_async_remote_copy(
            own.at[chan], nxt.at[chan], send_halo.at[1], recv_next.at[2 * chan],
            device_id=((depth + DEPTH - 1) % DEPTH, chan), device_id_type=MESH,
        )

    def tell(n, *devices):
        for device in devices:
            greet(device, know.at[n])

    def hear(n, count=2):
        pl.semaphore_wait(know.at[n], count)

    def neighbours():
        when(greets_up | greets_down, hear, 0, 1)
        when(y == 0, hear, 7, 2)
        when(y % 2 == 1, hear, 7, 1)
        tell(1, *up(1))

    def two_away():
        hear(1)
        tell(2, *up(2))

    def four_away():
        hear(2)
        tell(3, partner)
        hear(3, 1)
        when((core == 1) & (zh < 3), lambda: plane_up().start())
        when((core == 0) & (zh > 0), lambda: shard_down().start())
        tell(4, *beside)

    def next_row():
        hear(4)
        when((core == 1) & (zh == 3) & (y < NY - 1), lambda: plane_up().start())
        when((core == 0) & (zh == 0) & (y > 0), lambda: shard_down().start())
        tell(5, *up(4))

    def all_rows():
        hear(5)
        tell(6, *beside)

    late = zh > 0
    early = zh == 0
    mine.begin()
    hand(chan)
    when(core == 0, lambda: plane_up().start())
    when(heard_down, tell, 0, up(1)[1])
    when(heard_up, tell, 0, up(1)[0])
    when(y % 2 == 1, tell, 7, at(x, 0, z, core))
    when(y == 2, tell, 7, *beside)
    mine.rows(1)
    when(late, neighbours)
    mine.turns(0)
    when(late, two_away)
    take_volume.wait()
    own_views(volume, views)
    mine.rows(2)
    when(late, four_away)
    mine.rows(3)
    mine.turns(1)
    when(late, next_row)
    mine.turns(2)
    when(early, neighbours)
    mine.turns(3)
    when(early, two_away)
    when(late, all_rows)
    when(early, four_away)
    mine.ends()
    when(early, next_row)
    when(depth > 0, lambda: plane_up().wait_recv())

    @pl.when(depth == 0)
    def _():
        halo[...] = jnp.zeros_like(halo)

    halo_views(halo, views)
    terms = kernel_terms(own, views)
    parts[:, 0] = terms[:, :4]
    parts[:, 1] = terms[:, 4:]
    when(early, all_rows)
    hear(6)
    for step in FAR_FIRST:
        dy, dz, dc = step // 8, (step // 2) % 4, step % 2
        peer = (((y + dy) % NY) * 4 + (zh + dz) % 4) * 2 + (core + dc) % 2
        pltpu.make_async_remote_copy(
            parts.at[peer // 2, peer % 2], arrived.at[step - 1], send_parts, recv_parts,
            device_id=(peer, chan), device_id_type=MESH,
        ).start()

    take_weight.wait()
    for_own, for_next = own_weights(weight, chan)
    gathers_next = (core == 1) & (depth < DEPTH - 1)

    @pl.when(gathers_next)
    def _():
        shard_down().wait_recv()
        after.begin()
        after.rows(1)
        after.turns(0)
        after.rows(2)
        after.rows(3)
        for k in range(1, 4):
            after.turns(k)
        after.ends()

    @pl.when(depth == DEPTH - 1)
    def _():
        nxt[...] = jnp.zeros_like(nxt)

    @pl.when(core == 0)
    def _():
        for slot in range(CHAN):
            to_partner(slot).wait_recv()

    planes = input_terms(own, nxt, for_own, for_next)
    for p in range(2):
        result[:, p] = planes[p]
    put = pltpu.make_async_copy(result, input_hbm, local.at[2])
    put.start()
    every_part = pltpu.make_async_remote_copy(
        arrived, arrived, send_parts, recv_parts, device_id=partner, device_id_type=MESH
    )
    every_part.wait_recv()
    total = parts[depth // 2, depth % 2] + jnp.sum(arrived[...], axis=0)
    total = total * (1.0 / math.sqrt(DEPTH * ROWS * COLS))
    turned = jnp.transpose(jnp.concatenate([total, total], axis=0))
    for a in range(3):
        for b in range(3):
            for e in range(3):
                c = column_of(a, b, e)
                kernel_ref[9 * a + 3 * b + e] = turned[c : c + 4, :4]
    mine.sent()
    when(gathers_next, after.sent)

    @pl.when(core == 1)
    def _():
        pltpu.make_async_remote_copy(
            own, nxt, send_chip, recv_next.at[0], device_id=partner, device_id_type=MESH
        ).wait_send()

    when(depth < DEPTH - 1, lambda: plane_up().wait_send())
    when((core == 0) & (depth > 0), lambda: shard_down().wait_send())
    every_part.wait_send()
    put.wait()


def shards(grad_out, volume, weight):
    any_space = pl.BlockSpec(memory_space=pl.ANY)
    in_vmem = pl.BlockSpec(memory_space=pltpu.VMEM)
    dma = pltpu.SemaphoreType.DMA
    plane = pltpu.VMEM((CHAN, 16, 16, COLS), BF16)
    return pl.pallas_call(
        body,
        out_shape=(
            jax.ShapeDtypeStruct(volume.shape, BF16),
            jax.ShapeDtypeStruct((27, CI, 4), F32),
        ),
        in_specs=[any_space, any_space, any_space],
        out_specs=(any_space, in_vmem),
        scratch_shapes=[
            plane,
            plane,
            pltpu.VMEM((16, 2, 8, 16, COLS), BF16),
            pltpu.VMEM(grad_out.shape, BF16),
            pltpu.VMEM(volume.shape, BF16),
            pltpu.VMEM((CI, 64, 256), BF16),
            pltpu.VMEM(weight.shape, BF16),
            pltpu.VMEM((16, 2, 4, 128), F32),
            pltpu.VMEM((DEPTH - 1, 4, 128), F32),
            pltpu.VMEM(volume.shape, BF16),
            dma((2 * CHAN,)),
            dma((2 * CHAN,)),
            dma,
            dma,
            dma((2,)),
            dma((2,)),
            dma,
            dma((2,)),
            dma,
            dma((4,)),
            pltpu.SemaphoreType.REGULAR((8,)),
        ],
        compiler_params=pltpu.CompilerParams(collective_id=0, has_side_effects=True),
    )(grad_out, volume, weight)


def solution(mesh):
    in_specs = (P("chan", "depth", None, None), P("chan", "depth", None, None), P())
    out_specs = (P("chan", "depth", None, None), P(None, "chan", "depth"))
    return jax.shard_map(shards, mesh=mesh, in_specs=in_specs, out_specs=out_specs, check_vma=False)
```

```python
import math

import jax
import jax.numpy as jnp
from jax import lax
from jax.experimental import pallas as pl
from jax.experimental.pallas import tpu as pltpu
from jax.sharding import PartitionSpec as P

MESH = pl.DeviceIdType.MESH
BF16 = jnp.bfloat16
F32 = jnp.float32
NX, NY, NZ, NZL, DEPTH, CHAN = 4, 4, 16, 4, 32, 16
CI, ROWS, COLS = 4, 32, 128
FAR_FIRST = sorted(range(1, 32), key=lambda n: -(4 * min(n // 2 % 4, 4 - n // 2 % 4) + min(n // 8, 4 - n // 8)))


def grid_of(shape):
    return lax.broadcasted_iota(jnp.int32, shape, 0), lax.broadcasted_iota(jnp.int32, shape, 1)


def picks(mask):
    return jnp.where(mask, 1.0, 0.0).astype(BF16)


def mm(a, b):
    return jnp.dot(a, b, preferred_element_type=F32)


def exact(a, b):
    return mm(a, b).astype(BF16)


def packed_shard(block):
    r, k = grid_of((256, 256))
    rows = picks(k == (r & 7) * 32 + ((r >> 3) & 1) * 16 + (r >> 4))
    return exact(rows, block.reshape(256, COLS)).reshape(16, 16, COLS)


def column_views(plane):
    l, k = grid_of((256, 384))
    return exact(plane.reshape(256, 256), picks(l == 2 * (k & 127) + (k >> 7) - 1))


def row_picker(offset_of, keep):
    row, k = grid_of((512, 256))
    h, r = row >> 4, row & 15
    hit = ((k >> 6) == (r & 3)) & ((k & 63) == 2 * h + offset_of(r)) & keep(r)
    return picks(hit)


def own_views(volume_ref, views_ref):
    picker = row_picker(lambda r: (r >> 2) - 1, lambda r: r < 12)
    for p in range(2):
        taken = exact(picker, column_views(volume_ref[:, p]))
        for s in range(2):
            for e in range(3):
                part = taken[256 * s : 256 * s + 256, 128 * e : 128 * e + 128]
                views_ref[:, s, 3 * p + e] = part.reshape(16, 16, COLS)


def halo_views(halo_ref, views_ref):
    columns = column_views(halo_ref[...])
    for b in range(2):
        taken = exact(row_picker(lambda r, b=b: b - 1, lambda r: r >= 12), columns)
        for s in range(2):
            for e in range(3):
                part = taken[256 * s : 256 * s + 256, 128 * e : 128 * e + 128]
                views_ref[:, s, 3 * b + e] += part.reshape(16, 16, COLS)
    last = jnp.zeros((512, COLS), F32)
    for e in range(3):
        picker = row_picker(lambda r: 1, lambda r, e=e: (r >> 2) == e)
        last = last + mm(picker, columns[:, 128 * e : 128 * e + 128])
    last = last.astype(BF16)
    for s in range(2):
        views_ref[:, s, 6] = last[256 * s : 256 * s + 256].reshape(16, 16, COLS)
        views_ref[:, s, 7] = jnp.zeros((16, 16, COLS), BF16)


def column_of(a, b, e):
    if a:
        return 16 * (3 * (a - 1) + e) + 4 * b
    return 16 * (3 * b + e) + 12 if b < 2 else 96 + 4 * e


def own_weights(weight_ref, chan):
    m, k = grid_of((144, 27 * 64))
    a, rest = m // 48, m % 48
    e, xy, slot, c = rest >> 4, (rest >> 3) & 1, (rest >> 2) & 1, rest & 3
    b = jnp.where(xy == 0, 1 + slot, 0)
    hit = (k == (9 * a + 3 * b + e) * 64 + CI * chan + c) & ((xy == 0) | (slot == 1))
    mine = exact(picks(hit), weight_ref[...].reshape(27 * 64, 128))
    o, k = grid_of((128, 256))
    spread = [exact(mine, picks((((k >> 3) & 1) == s) & (o == (k >> 4) * 8 + (k & 7)))) for s in range(2)]
    for_own = jnp.concatenate([spread[0][48:], spread[1][48:]], axis=0)
    for_next = jnp.concatenate([spread[0][:48], spread[1][:48]], axis=0)
    return for_own, for_next


def plane_of(ref):
    return jnp.concatenate([ref[:, hh].reshape(256, COLS) for hh in range(16)], axis=1)


def views_of(ref):
    return jnp.concatenate([ref[hh].reshape(256, COLS) for hh in range(16)], axis=1)


def kernel_terms(own_ref, views_ref):
    both = lax.dot_general(
        plane_of(own_ref), views_of(views_ref), (((1,), (1,)), ((), ())), preferred_element_type=F32
    ).reshape(16, 16, 256)
    return both[:, :8, :128] + both[:, 8:, 128:]


def input_terms(own_ref, next_ref, for_own, for_next):
    from_own = mm(for_own, plane_of(own_ref))
    from_next = mm(for_next, plane_of(next_ref))
    nothing = jnp.zeros((8, COLS), F32)
    w = lax.broadcasted_iota(jnp.int32, (8, 2048), 1) & 127

    def tap(product, tiles, tile, s):
        at = 16 * (s * tiles + tile)
        above = product[at + 8 : at + 16, COLS:]
        if s == 0:
            crossing = product[16 * tiles + 16 * tile + 8 : 16 * tiles + 16 * tile + 16, :COLS]
        else:
            crossing = nothing
        return product[at : at + 8] + jnp.concatenate([above, crossing], axis=1)

    r, k = grid_of((256, 256))
    lanes = picks(k == 2 * (r & 127) + (r >> 7))
    rows = picks(((r >> 6) == (k & 3)) & ((r & 63) == 2 * (k >> 3) + ((k >> 2) & 1)))
    planes = []
    for p in range(2):
        halves = []
        for s in range(2):
            by_e = [tap(from_own, 6, 3 * p + e, s) for e in range(3)]
            if p == 1:
                by_e = [by_e[e] + tap(from_next, 3, e, s) for e in range(3)]
            shifted = jnp.where(w == 127, 0.0, pltpu.roll(by_e[0], 2047, 1))
            even, odd = by_e[1], by_e[2] + shifted
            halves.append(
                jnp.concatenate(
                    [
                        jnp.concatenate([v[:, COLS * hh : COLS * hh + COLS] for hh in range(16)], axis=0)
                        for v in (even, odd)
                    ],
                    axis=1,
                )
            )
        mixed = jnp.concatenate(halves, axis=0).astype(BF16)
        planes.append(exact(rows, exact(mixed, lanes)).reshape(CI, 64, 256))
    return planes


def body(
    grad_hbm, volume_hbm, weight_hbm, input_hbm, kernel_ref,
    own, nxt, views, grad, volume, halo, weight, parts, arrived, result,
    recv_own, recv_next, recv_halo, recv_parts,
    send_x, send_z, send_chip, send_halo, send_parts, local, know,
):
    depth, chan = lax.axis_index("depth"), lax.axis_index("chan")
    core, zh, y = depth % 2, (depth // 2) % 4, depth // 8
    x, zl = chan % NX, chan // NX
    z = zh * NZL + zl

    def at(x_, y_, z_, core_):
        return ((y_ * 4 + z_ // NZL) * 2 + core_, (z_ % NZL) * NX + x_)

    xr, xl, x2 = (x + 1) % NX, (x + 3) % NX, (x + 2) % NX
    right, left = (depth, zl * NX + xr), (depth, zl * NX + xl)
    partner = (depth + 1 - 2 * core, chan)
    far = (depth, zl * NX + x2)
    row = (zl, zl + 1 - 2 * (zl % 2), (zl + 2) % NZL, NZL - 1 - zl)
    column = tuple((depth, v * NX + x) for v in row)
    here = tuple(v * NX + x for v in row)
    others = tuple(tuple(v * NX + c for c in (xl, xr, x2)) for v in row)

    def up(n):
        return at(x, y, (z + n) % NZ, core), at(x, y, (z + NZ - n) % NZ, core)

    beside = (at(x, (y + 1) % NY, z, core), at(x, (y + 3) % NY, z, core))

    barrier = pltpu.get_barrier_semaphore()

    def greet(device, sem=barrier):
        pl.semaphore_signal(sem, inc=1, device_id=device, device_id_type=MESH)

    def when(condition, act, *args):
        pl.when(condition)(lambda: act(*args))

    for device in (far, right, left, *column[1:], partner):
        greet(device)
    take_grad = pltpu.make_async_copy(grad_hbm, grad, local.at[3])
    take_grad.start()
    above, below = ((depth + 1) % DEPTH, chan), ((depth + DEPTH - 1) % DEPTH, chan)
    has_above, has_below = depth < DEPTH - 1, depth > 0
    calls_above, calls_below = (core == 1) & (zh < 3), (core == 0) & (zh == 0) & has_below
    heard_below, heard_above = (core == 0) & (zh > 0), (core == 1) & (zh == 3) & has_above
    greets_up, greets_down = (zl == 3) & (zh < 3), z == 0
    heard_down, heard_up = (zl == 0) & (zh > 0), z == NZ - 1
    when(calls_above, greet, above)
    when(calls_below, greet, below)
    when(greets_up, greet, up(1)[0])
    when(greets_down, greet, up(1)[1])
    when(y != 2, greet, at(x, y + 1 - 2 * (y // 3), z, core))
    when(y == 0, greet, beside[1])
    take_volume = pltpu.make_async_copy(volume_hbm, volume, local.at[0])
    take_weight = pltpu.make_async_copy(weight_hbm, weight, local.at[1])
    take_volume.start()
    take_weight.start()
    take_grad.wait()
    own[chan] = packed_shard(grad[...].reshape(8, ROWS, COLS))
    greeted = 7 + jnp.where(heard_down | heard_up, 1, 0)
    greeted = greeted + jnp.where(y == 2, 2, y % 2) + jnp.where(heard_below | heard_above, 1, 0)
    pl.semaphore_wait(barrier, greeted)

    class Plane:
        def __init__(self, ref, recv, n):
            self.ref, self.recv, self.n = ref, recv, n

        def copy(self, slot, device, sem):
            return pltpu.make_async_remote_copy(
                self.ref.at[slot], self.ref.at[slot], sem.at[self.n], self.recv.at[slot],
                device_id=device, device_id_type=MESH,
            )

        def sides(self, slot):
            for device in (far, right, left):
                self.copy(slot, device, send_x).start()

        def begin(self):
            self.sides(chan)
            for k in range(1, 4):
                self.copy(chan, column[k], send_z).start()

        def wait(self, slot):
            self.copy(slot, partner, send_x).wait_recv()

        def drained(self, sem, count):
            shards_ = self.ref.at[pl.ds(0, count)]
            pltpu.make_async_remote_copy(
                shards_, shards_, sem.at[self.n], self.recv.at[0], device_id=partner, device_id_type=MESH
            ).wait_send()

        def sent(self):
            self.drained(send_x, 12)
            self.drained(send_z, 3)

    def to_partner(slot):
        return pltpu.make_async_remote_copy(
            own.at[slot], nxt.at[slot], send_chip, recv_next.at[slot],
            device_id=partner, device_id_type=MESH,
        )

    def hand(slot):
        when(core == 1, lambda: to_partner(slot).start())

    mine, after = Plane(own, recv_own, 0), Plane(nxt, recv_next, 1)

    def row_at(k):
        mine.wait(here[k])
        mine.sides(here[k])
        hand(here[k])

    def rest_of(k):
        for slot in others[k]:
            mine.wait(slot)
            hand(slot)

    def plane_up():
        return pltpu.make_async_remote_copy(
            volume_hbm.at[:, 1], halo, send_halo.at[0], recv_halo,
            device_id=((depth + 1) % DEPTH, chan), device_id_type=MESH,
        )

    def shard_down():
        return pltpu.make_async_remote_copy(
            own.at[chan], nxt.at[chan], send_halo.at[1], recv_next.at[chan],
            device_id=((depth + DEPTH - 1) % DEPTH, chan), device_id_type=MESH,
        )

    def tell(n, *devices):
        for device in devices:
            greet(device, know.at[n])

    def hear(n, count=2):
        pl.semaphore_wait(know.at[n], count)

    def neighbours():
        when(greets_up | greets_down, hear, 0, 1)
        when(y == 0, hear, 7, 2)
        when(y % 2 == 1, hear, 7, 1)
        tell(1, *up(1))

    def two_away():
        hear(1)
        tell(2, *up(2))

    def four_away():
        hear(2)
        tell(3, partner)
        hear(3, 1)
        tell(4, *beside)

    def next_row():
        hear(4)
        tell(5, *up(4))

    def all_rows():
        hear(5)
        tell(6, *beside)

    def trade_down():
        hear(8, 1)
        shard_down().start()

    def trade_up():
        hear(8, 1)
        plane_up().start()

    def next_rows():
        shard_down().wait_recv()
        after.begin()
        for k in range(1, 4):
            after.wait(here[k])
            after.sides(here[k])

    late, early = zh > 0, zh == 0
    gathers_next = (core == 1) & has_above
    mine.begin()
    hand(chan)
    when(core == 0, lambda: plane_up().start())
    when(heard_below, tell, 8, below)
    when(heard_above, tell, 8, above)
    when(heard_down, tell, 0, up(1)[1])
    when(heard_up, tell, 0, up(1)[0])
    when(y % 2 == 1, tell, 7, at(x, 0, z, core))
    when(y == 2, tell, 7, *beside)
    when(heard_below, lambda: shard_down().start())
    row_at(1)
    when(late, neighbours)
    row_at(2)
    when(late, two_away)
    row_at(3)
    when(early, neighbours)
    take_volume.wait()
    own_views(volume, views)
    when(heard_above, lambda: plane_up().start())
    when(calls_above, trade_up)
    when(early, two_away)
    four_away()
    when(calls_below, trade_down)
    rest_of(0)
    next_row()
    rest_of(1)
    when(has_below, lambda: plane_up().wait_recv())

    @pl.when(depth == 0)
    def _():
        halo[...] = jnp.zeros_like(halo)

    halo_views(halo, views)
    when(gathers_next & (zh < 2), next_rows)
    rest_of(2)
    all_rows()
    rest_of(3)
    terms = kernel_terms(own, views)
    parts[:, 0] = terms[:, :4]
    parts[:, 1] = terms[:, 4:]
    hear(6)
    for step in FAR_FIRST:
        dy, dz, dc = step // 8, (step // 2) % 4, step % 2
        peer = (((y + dy) % NY) * 4 + (zh + dz) % 4) * 2 + (core + dc) % 2
        pltpu.make_async_remote_copy(
            parts.at[peer // 2, peer % 2], arrived.at[step - 1], send_parts, recv_parts,
            device_id=(peer, chan), device_id_type=MESH,
        ).start()

    take_weight.wait()
    for_own, for_next = own_weights(weight, chan)
    when(gathers_next & (zh >= 2), next_rows)

    @pl.when(gathers_next)
    def _():
        for k in range(4):
            for slot in others[k]:
                after.wait(slot)

    @pl.when(depth == DEPTH - 1)
    def _():
        nxt[...] = jnp.zeros_like(nxt)

    @pl.when(core == 0)
    def _():
        for slot in range(CHAN):
            to_partner(slot).wait_recv()

    planes = input_terms(own, nxt, for_own, for_next)
    for p in range(2):
        result[:, p] = planes[p]
    put = pltpu.make_async_copy(result, input_hbm, local.at[2])
    put.start()
    every_part = pltpu.make_async_remote_copy(
        arrived, arrived, send_parts, recv_parts, device_id=partner, device_id_type=MESH
    )
    every_part.wait_recv()
    total = parts[depth // 2, depth % 2] + jnp.sum(arrived[...], axis=0)
    total = total * (1.0 / math.sqrt(DEPTH * ROWS * COLS))
    turned = jnp.transpose(jnp.concatenate([total, total], axis=0))
    for a in range(3):
        for b in range(3):
            for e in range(3):
                c = column_of(a, b, e)
                kernel_ref[9 * a + 3 * b + e] = turned[c : c + 4, :4]
    mine.sent()
    when(gathers_next, after.sent)

    @pl.when(core == 1)
    def _():
        pltpu.make_async_remote_copy(
            own, nxt, send_chip, recv_next.at[0], device_id=partner, device_id_type=MESH
        ).wait_send()

    when(depth < DEPTH - 1, lambda: plane_up().wait_send())
    when((core == 0) & (depth > 0), lambda: shard_down().wait_send())
    every_part.wait_send()
    put.wait()


def shards(grad_out, volume, weight):
    any_space = pl.BlockSpec(memory_space=pl.ANY)
    in_vmem = pl.BlockSpec(memory_space=pltpu.VMEM)
    dma = pltpu.SemaphoreType.DMA
    plane = pltpu.VMEM((CHAN, 16, 16, COLS), BF16)
    return pl.pallas_call(
        body,
        out_shape=(
            jax.ShapeDtypeStruct(volume.shape, BF16),
            jax.ShapeDtypeStruct((27, CI, 4), F32),
        ),
        in_specs=[any_space, any_space, any_space],
        out_specs=(any_space, in_vmem),
        scratch_shapes=[
            plane,
            plane,
            pltpu.VMEM((16, 2, 8, 16, COLS), BF16),
            pltpu.VMEM(grad_out.shape, BF16),
            pltpu.VMEM(volume.shape, BF16),
            pltpu.VMEM((CI, 64, 256), BF16),
            pltpu.VMEM(weight.shape, BF16),
            pltpu.VMEM((16, 2, 4, 128), F32),
            pltpu.VMEM((DEPTH - 1, 4, 128), F32),
            pltpu.VMEM(volume.shape, BF16),
            dma((CHAN,)),
            dma((CHAN,)),
            dma,
            dma,
            dma((2,)),
            dma((2,)),
            dma,
            dma((2,)),
            dma,
            dma((4,)),
            pltpu.SemaphoreType.REGULAR((9,)),
        ],
        compiler_params=pltpu.CompilerParams(collective_id=0, has_side_effects=True),
    )(grad_out, volume, weight)


def solution(mesh):
    in_specs = (P("chan", "depth", None, None), P("chan", "depth", None, None), P())
    out_specs = (P("chan", "depth", None, None), P(None, "chan", "depth"))
    return jax.shard_map(shards, mesh=mesh, in_specs=in_specs, out_specs=out_specs, check_vma=False)
```

```python
import math

import jax
import jax.numpy as jnp
from jax import lax
from jax.experimental import pallas as pl
from jax.experimental.pallas import tpu as pltpu
from jax.sharding import PartitionSpec as P

MESH = pl.DeviceIdType.MESH
BF16 = jnp.bfloat16
F32 = jnp.float32
NX, NY, NZ, NZL, DEPTH, CHAN = 4, 4, 16, 4, 32, 16
CI, ROWS, COLS = 4, 32, 128
FAR_FIRST = sorted(range(1, 32), key=lambda n: -(4 * min(n // 2 % 4, 4 - n // 2 % 4) + min(n // 8, 4 - n // 8)))


def grid_of(shape):
    return lax.broadcasted_iota(jnp.int32, shape, 0), lax.broadcasted_iota(jnp.int32, shape, 1)


def picks(mask):
    return jnp.where(mask, 1.0, 0.0).astype(BF16)


def mm(a, b):
    return jnp.dot(a, b, preferred_element_type=F32)


def exact(a, b):
    return mm(a, b).astype(BF16)


def packed_shard(block):
    r, k = grid_of((256, 256))
    rows = picks(k == (r & 7) * 32 + ((r >> 3) & 1) * 16 + (r >> 4))
    return exact(rows, block.reshape(256, COLS)).reshape(16, 16, COLS)


def column_views(plane):
    l, k = grid_of((256, 384))
    return exact(plane.reshape(256, 256), picks(l == 2 * (k & 127) + (k >> 7) - 1))


def row_picker(offset_of, keep):
    row, k = grid_of((512, 256))
    h, r = row >> 4, row & 15
    hit = ((k >> 6) == (r & 3)) & ((k & 63) == 2 * h + offset_of(r)) & keep(r)
    return picks(hit)


def own_views(volume_ref, views_ref):
    picker = row_picker(lambda r: (r >> 2) - 1, lambda r: r < 12)
    for p in range(2):
        taken = exact(picker, column_views(volume_ref[:, p]))
        for s in range(2):
            for e in range(3):
                part = taken[256 * s : 256 * s + 256, 128 * e : 128 * e + 128]
                views_ref[:, s, 3 * p + e] = part.reshape(16, 16, COLS)


def halo_views(halo_ref, views_ref):
    columns = column_views(halo_ref[...])
    for b in range(2):
        taken = exact(row_picker(lambda r, b=b: b - 1, lambda r: r >= 12), columns)
        for s in range(2):
            for e in range(3):
                part = taken[256 * s : 256 * s + 256, 128 * e : 128 * e + 128]
                views_ref[:, s, 3 * b + e] += part.reshape(16, 16, COLS)
    last = jnp.zeros((512, COLS), F32)
    for e in range(3):
        picker = row_picker(lambda r: 1, lambda r, e=e: (r >> 2) == e)
        last = last + mm(picker, columns[:, 128 * e : 128 * e + 128])
    last = last.astype(BF16)
    for s in range(2):
        views_ref[:, s, 6] = last[256 * s : 256 * s + 256].reshape(16, 16, COLS)
        views_ref[:, s, 7] = jnp.zeros((16, 16, COLS), BF16)


def column_order():
    col, k = grid_of((128, 128))
    c, t = k >> 5, k & 31
    a, b, e = t // 9, (t // 3) % 3, t % 3
    source = jnp.where(a > 0, 16 * (3 * a - 3 + e) + 4 * b, jnp.where(b < 2, 16 * (3 * b + e) + 12, 96 + 4 * e))
    return jnp.where((col == source + c) & (t < 27), 1.0, 0.0)


def own_weights(weight_ref, chan):
    m, k = grid_of((144, 27 * 64))
    a, rest = m // 48, m % 48
    e, xy, slot, c = rest >> 4, (rest >> 3) & 1, (rest >> 2) & 1, rest & 3
    b = jnp.where(xy == 0, 1 + slot, 0)
    hit = (k == (9 * a + 3 * b + e) * 64 + CI * chan + c) & ((xy == 0) | (slot == 1))
    mine = exact(picks(hit), weight_ref[...].reshape(27 * 64, 128))
    o, k = grid_of((128, 256))
    spread = [exact(mine, picks((((k >> 3) & 1) == s) & (o == (k >> 4) * 8 + (k & 7)))) for s in range(2)]
    for_own = jnp.concatenate([spread[0][48:], spread[1][48:]], axis=0)
    for_next = jnp.concatenate([spread[0][:48], spread[1][:48]], axis=0)
    return for_own, for_next


def plane_of(ref):
    return jnp.concatenate([ref[:, hh].reshape(256, COLS) for hh in range(16)], axis=1)


def views_of(ref):
    return jnp.concatenate([ref[hh].reshape(256, COLS) for hh in range(16)], axis=1)


def kernel_terms(own_ref, views_ref):
    both = lax.dot_general(
        plane_of(own_ref), views_of(views_ref), (((1,), (1,)), ((), ())), preferred_element_type=F32
    ).reshape(16, 16, 256)
    return both[:, :8, :128] + both[:, 8:, 128:]


def input_terms(own_ref, next_ref, for_own, for_next):
    from_own = mm(for_own, plane_of(own_ref))
    from_next = mm(for_next, plane_of(next_ref))
    nothing = jnp.zeros((8, COLS), F32)
    w = lax.broadcasted_iota(jnp.int32, (8, 2048), 1) & 127

    def tap(product, tiles, tile, s):
        at = 16 * (s * tiles + tile)
        above = product[at + 8 : at + 16, COLS:]
        if s == 0:
            crossing = product[16 * tiles + 16 * tile + 8 : 16 * tiles + 16 * tile + 16, :COLS]
        else:
            crossing = nothing
        return product[at : at + 8] + jnp.concatenate([above, crossing], axis=1)

    r, k = grid_of((256, 256))
    lanes = picks(k == 2 * (r & 127) + (r >> 7))
    rows = picks(((r >> 6) == (k & 3)) & ((r & 63) == 2 * (k >> 3) + ((k >> 2) & 1)))
    planes = []
    for p in range(2):
        halves = []
        for s in range(2):
            by_e = [tap(from_own, 6, 3 * p + e, s) for e in range(3)]
            if p == 1:
                by_e = [by_e[e] + tap(from_next, 3, e, s) for e in range(3)]
            shifted = jnp.where(w == 127, 0.0, pltpu.roll(by_e[0], 2047, 1))
            even, odd = by_e[1], by_e[2] + shifted
            halves.append(
                jnp.concatenate(
                    [
                        jnp.concatenate([v[:, COLS * hh : COLS * hh + COLS] for hh in range(16)], axis=0)
                        for v in (even, odd)
                    ],
                    axis=1,
                )
            )
        mixed = jnp.concatenate(halves, axis=0).astype(BF16)
        planes.append(exact(rows, exact(mixed, lanes)).reshape(CI, 64, 256))
    return planes


def body(
    grad_hbm, volume_hbm, weight_hbm, result, kernel_ref,
    own, nxt, views, grad, volume, halo, weight, parts, arrived,
    recv_own, recv_next, recv_halo, recv_parts,
    send_x, send_z, send_chip, send_halo, send_parts, local, know,
):
    depth, chan = lax.axis_index("depth"), lax.axis_index("chan")
    core, zh, y = depth % 2, (depth // 2) % 4, depth // 8
    x, zl = chan % NX, chan // NX
    z = zh * NZL + zl

    def at(x_, y_, z_, core_):
        return ((y_ * 4 + z_ // NZL) * 2 + core_, (z_ % NZL) * NX + x_)

    xr, xl, x2 = (x + 1) % NX, (x + 3) % NX, (x + 2) % NX
    right, left = (depth, zl * NX + xr), (depth, zl * NX + xl)
    partner = (depth + 1 - 2 * core, chan)
    far = (depth, zl * NX + x2)
    row = (zl, zl + 1 - 2 * (zl % 2), (zl + 2) % NZL, NZL - 1 - zl)
    column = tuple((depth, v * NX + x) for v in row)
    here = tuple(v * NX + x for v in row)
    others = tuple(tuple(v * NX + c for c in (xl, xr, x2)) for v in row)

    def up(n):
        return at(x, y, (z + n) % NZ, core), at(x, y, (z + NZ - n) % NZ, core)

    beside = (at(x, (y + 1) % NY, z, core), at(x, (y + 3) % NY, z, core))

    barrier = pltpu.get_barrier_semaphore()

    def greet(device, sem=barrier):
        pl.semaphore_signal(sem, inc=1, device_id=device, device_id_type=MESH)

    def when(condition, act, *args):
        pl.when(condition)(lambda: act(*args))

    for device in (far, right, left, *column[1:], partner):
        greet(device)
    take_grad = pltpu.make_async_copy(grad_hbm, grad, local.at[3])
    take_grad.start()
    above, below = ((depth + 1) % DEPTH, chan), ((depth + DEPTH - 1) % DEPTH, chan)
    has_above, has_below = depth < DEPTH - 1, depth > 0
    calls_above, calls_below = (core == 1) & (zh < 3), (core == 0) & (zh == 0) & has_below
    heard_below, heard_above = (core == 0) & (zh > 0), (core == 1) & (zh == 3) & has_above
    greets_up, greets_down = (zl == 3) & (zh < 3), z == 0
    heard_down, heard_up = (zl == 0) & (zh > 0), z == NZ - 1
    when(calls_above, greet, above)
    when(calls_below, greet, below)
    when(greets_up, greet, up(1)[0])
    when(greets_down, greet, up(1)[1])
    when(y != 2, greet, at(x, y + 1 - 2 * (y // 3), z, core))
    when(y == 0, greet, beside[1])
    take_volume = pltpu.make_async_copy(volume_hbm, volume, local.at[0])
    take_weight = pltpu.make_async_copy(weight_hbm, weight, local.at[1])
    take_volume.start()
    take_weight.start()
    take_grad.wait()
    own[chan] = packed_shard(grad[...].reshape(8, ROWS, COLS))
    greeted = 7 + jnp.where(heard_down | heard_up, 1, 0)
    greeted = greeted + jnp.where(y == 2, 2, y % 2) + jnp.where(heard_below | heard_above, 1, 0)
    pl.semaphore_wait(barrier, greeted)

    class Plane:
        def __init__(self, ref, recv, n):
            self.ref, self.recv, self.n = ref, recv, n

        def copy(self, slot, device, sem):
            return pltpu.make_async_remote_copy(
                self.ref.at[slot], self.ref.at[slot], sem.at[self.n], self.recv.at[slot],
                device_id=device, device_id_type=MESH,
            )

        def sides(self, slot):
            for device in (far, right, left):
                self.copy(slot, device, send_x).start()

        def begin(self):
            self.sides(chan)
            for k in range(1, 4):
                self.copy(chan, column[k], send_z).start()

        def wait(self, slot):
            self.copy(slot, partner, send_x).wait_recv()

        def drained(self, sem, count):
            shards_ = self.ref.at[pl.ds(0, count)]
            pltpu.make_async_remote_copy(
                shards_, shards_, sem.at[self.n], self.recv.at[0], device_id=partner, device_id_type=MESH
            ).wait_send()

        def sent(self):
            self.drained(send_x, 12)
            self.drained(send_z, 3)

    def to_partner(slot):
        return pltpu.make_async_remote_copy(
            own.at[slot], nxt.at[slot], send_chip, recv_next.at[slot],
            device_id=partner, device_id_type=MESH,
        )

    def hand(slot):
        when(core == 1, lambda: to_partner(slot).start())

    mine, after = Plane(own, recv_own, 0), Plane(nxt, recv_next, 1)

    def row_at(k):
        mine.wait(here[k])
        mine.sides(here[k])
        hand(here[k])

    def rest_of(k):
        for slot in others[k]:
            mine.wait(slot)
            hand(slot)

    def plane_up():
        return pltpu.make_async_remote_copy(
            volume_hbm.at[:, 1], halo, send_halo.at[0], recv_halo,
            device_id=((depth + 1) % DEPTH, chan), device_id_type=MESH,
        )

    def shard_down():
        return pltpu.make_async_remote_copy(
            own.at[chan], nxt.at[chan], send_halo.at[1], recv_next.at[chan],
            device_id=((depth + DEPTH - 1) % DEPTH, chan), device_id_type=MESH,
        )

    def tell(n, *devices):
        for device in devices:
            greet(device, know.at[n])

    def hear(n, count=2):
        pl.semaphore_wait(know.at[n], count)

    def neighbours():
        when(greets_up | greets_down, hear, 0, 1)
        when(y == 0, hear, 7, 2)
        when(y % 2 == 1, hear, 7, 1)
        tell(1, *up(1))

    def two_away():
        hear(1)
        tell(2, *up(2))

    def four_away():
        hear(2)
        tell(3, partner)
        hear(3, 1)
        tell(4, *beside)

    def next_row():
        hear(4)
        tell(5, *up(4))

    def all_rows():
        hear(5)
        tell(6, *beside)

    def trade_down():
        hear(8, 1)
        shard_down().start()

    def trade_up():
        hear(8, 1)
        plane_up().start()

    def next_rows():
        shard_down().wait_recv()
        after.begin()
        for k in range(1, 4):
            after.wait(here[k])
            after.sides(here[k])

    late, early = zh > 0, zh == 0
    gathers_next = (core == 1) & has_above
    mine.begin()
    hand(chan)
    when(core == 0, lambda: plane_up().start())
    when(heard_below, tell, 8, below)
    when(heard_above, tell, 8, above)
    when(heard_down, tell, 0, up(1)[1])
    when(heard_up, tell, 0, up(1)[0])
    when(y % 2 == 1, tell, 7, at(x, 0, z, core))
    when(y == 2, tell, 7, *beside)
    when(heard_below, lambda: shard_down().start())
    row_at(1)
    when(late, neighbours)
    row_at(2)
    when(late, two_away)
    row_at(3)
    when(early, neighbours)
    take_volume.wait()
    own_views(volume, views)
    when(heard_above, lambda: plane_up().start())
    when(calls_above, trade_up)
    when(early, two_away)
    four_away()
    when(calls_below, trade_down)
    rest_of(0)
    next_row()
    rest_of(1)
    when(has_below, lambda: plane_up().wait_recv())

    @pl.when(depth == 0)
    def _():
        halo[...] = jnp.zeros_like(halo)

    halo_views(halo, views)
    when(gathers_next & (zh < 2), next_rows)
    rest_of(2)
    all_rows()
    rest_of(3)
    terms = kernel_terms(own, views)
    parts[:, 0] = terms[:, :4]
    parts[:, 1] = terms[:, 4:]
    hear(6)
    for step in FAR_FIRST:
        dy, dz, dc = step // 8, (step // 2) % 4, step % 2
        peer = (((y + dy) % NY) * 4 + (zh + dz) % 4) * 2 + (core + dc) % 2
        pltpu.make_async_remote_copy(
            parts.at[peer // 2, peer % 2], arrived.at[step - 1], send_parts, recv_parts,
            device_id=(peer, chan), device_id_type=MESH,
        ).start()

    take_weight.wait()
    for_own, for_next = own_weights(weight, chan)
    when(gathers_next & (zh >= 2), next_rows)

    @pl.when(gathers_next)
    def _():
        for k in range(4):
            for slot in others[k]:
                after.wait(slot)

    @pl.when(depth == DEPTH - 1)
    def _():
        nxt[...] = jnp.zeros_like(nxt)

    @pl.when(core == 0)
    def _():
        for slot in range(CHAN):
            to_partner(slot).wait_recv()

    planes = input_terms(own, nxt, for_own, for_next)
    for p in range(2):
        result[:, p] = planes[p]
    choose = column_order()
    every_part = pltpu.make_async_remote_copy(
        arrived, arrived, send_parts, recv_parts, device_id=partner, device_id_type=MESH
    )
    every_part.wait_recv()
    total = parts[depth // 2, depth % 2] + jnp.sum(arrived[...], axis=0)
    chosen = jnp.dot(
        jnp.concatenate([total, total], axis=0), choose, precision=lax.Precision.HIGHEST, preferred_element_type=F32
    )
    chosen = chosen * (1.0 / math.sqrt(DEPTH * ROWS * COLS))
    for c in range(CI):
        kernel_ref[c] = chosen[:4, 32 * c : 32 * c + 27]
    mine.sent()
    when(gathers_next, after.sent)

    @pl.when(core == 1)
    def _():
        pltpu.make_async_remote_copy(
            own, nxt, send_chip, recv_next.at[0], device_id=partner, device_id_type=MESH
        ).wait_send()

    when(depth < DEPTH - 1, lambda: plane_up().wait_send())
    when((core == 0) & (depth > 0), lambda: shard_down().wait_send())
    every_part.wait_send()


def shards(grad_out, volume, weight):
    any_space = pl.BlockSpec(memory_space=pl.ANY)
    in_vmem = pl.BlockSpec(memory_space=pltpu.VMEM)
    dma = pltpu.SemaphoreType.DMA
    plane = pltpu.VMEM((CHAN, 16, 16, COLS), BF16)
    input_grad, kernel_grad = pl.pallas_call(
        body,
        out_shape=(pltpu.VMEM(volume.shape, BF16), pltpu.VMEM((CI, 4, 27), F32)),
        in_specs=[any_space, any_space, any_space],
        out_specs=(in_vmem, in_vmem),
        scratch_shapes=[
            plane,
            plane,
            pltpu.VMEM((16, 2, 8, 16, COLS), BF16),
            pltpu.VMEM(grad_out.shape, BF16),
            pltpu.VMEM(volume.shape, BF16),
            pltpu.VMEM((CI, 64, 256), BF16),
            pltpu.VMEM(weight.shape, BF16),
            pltpu.VMEM((16, 2, 4, 128), F32),
            pltpu.VMEM((DEPTH - 1, 4, 128), F32),
            dma((CHAN,)),
            dma((CHAN,)),
            dma,
            dma,
            dma((2,)),
            dma((2,)),
            dma,
            dma((2,)),
            dma,
            dma((4,)),
            pltpu.SemaphoreType.REGULAR((9,)),
        ],
        compiler_params=pltpu.CompilerParams(collective_id=0, has_side_effects=True),
    )(grad_out, volume, weight)
    return input_grad, jnp.transpose(kernel_grad, (2, 0, 1))


def solution(mesh):
    in_specs = (P("chan", "depth", None, None), P("chan", "depth", None, None), P())
    out_specs = (P("chan", "depth", None, None), P(None, "chan", "depth"))
    return jax.shard_map(shards, mesh=mesh, in_specs=in_specs, out_specs=out_specs, check_vma=False)
```

```python
import math

import jax
import jax.numpy as jnp
from jax import lax
from jax.experimental import pallas as pl
from jax.experimental.pallas import tpu as pltpu
from jax.sharding import PartitionSpec as P

MESH = pl.DeviceIdType.MESH
BF16 = jnp.bfloat16
F32 = jnp.float32
NX, NY, NZ, NZL, DEPTH, CHAN = 4, 4, 16, 4, 32, 16
CI, ROWS, COLS = 4, 32, 128
FAR_FIRST = sorted(range(1, 32), key=lambda n: -(4 * min(n // 2 % 4, 4 - n // 2 % 4) + min(n // 8, 4 - n // 8)))


def grid_of(shape):
    return lax.broadcasted_iota(jnp.int32, shape, 0), lax.broadcasted_iota(jnp.int32, shape, 1)


def picks(mask):
    return jnp.where(mask, 1.0, 0.0).astype(BF16)


def mm(a, b):
    return jnp.dot(a, b, preferred_element_type=F32)


def exact(a, b):
    return mm(a, b).astype(BF16)


def packed_shard(block):
    r, k = grid_of((256, 256))
    rows = picks(k == (r & 7) * 32 + ((r >> 3) & 1) * 16 + (r >> 4))
    return exact(rows, block.reshape(256, COLS)).reshape(16, 16, COLS)


def column_views(plane):
    l, k = grid_of((256, 384))
    return exact(plane.reshape(256, 256), picks(l == 2 * (k & 127) + (k >> 7) - 1))


def row_picker(offset_of, keep):
    row, k = grid_of((512, 256))
    h, r = row >> 4, row & 15
    hit = ((k >> 6) == (r & 3)) & ((k & 63) == 2 * h + offset_of(r)) & keep(r)
    return picks(hit)


def own_views(volume_ref, views_ref):
    picker = row_picker(lambda r: (r >> 2) - 1, lambda r: r < 12)
    for p in range(2):
        taken = exact(picker, column_views(volume_ref[:, p]))
        for s in range(2):
            for e in range(3):
                part = taken[256 * s : 256 * s + 256, 128 * e : 128 * e + 128]
                views_ref[:, s, 3 * p + e] = part.reshape(16, 16, COLS)


def halo_views(halo_ref, views_ref):
    columns = column_views(halo_ref[...])
    for b in range(2):
        taken = exact(row_picker(lambda r, b=b: b - 1, lambda r: r >= 12), columns)
        for s in range(2):
            for e in range(3):
                part = taken[256 * s : 256 * s + 256, 128 * e : 128 * e + 128]
                views_ref[:, s, 3 * b + e] += part.reshape(16, 16, COLS)
    last = jnp.zeros((512, COLS), F32)
    for e in range(3):
        picker = row_picker(lambda r: 1, lambda r, e=e: (r >> 2) == e)
        last = last + mm(picker, columns[:, 128 * e : 128 * e + 128])
    last = last.astype(BF16)
    for s in range(2):
        views_ref[:, s, 6] = last[256 * s : 256 * s + 256].reshape(16, 16, COLS)
        views_ref[:, s, 7] = jnp.zeros((16, 16, COLS), BF16)


def column_order():
    col, k = grid_of((128, 128))
    c, t = k >> 5, k & 31
    a, b, e = t // 9, (t // 3) % 3, t % 3
    source = jnp.where(a > 0, 16 * (3 * a - 3 + e) + 4 * b, jnp.where(b < 2, 16 * (3 * b + e) + 12, 96 + 4 * e))
    return jnp.where((col == source + c) & (t < 27), 1.0, 0.0)


def own_weights(weight_ref, chan):
    m, k = grid_of((144, 27 * 64))
    a, rest = m // 48, m % 48
    e, xy, slot, c = rest >> 4, (rest >> 3) & 1, (rest >> 2) & 1, rest & 3
    b = jnp.where(xy == 0, 1 + slot, 0)
    hit = (k == (9 * a + 3 * b + e) * 64 + CI * chan + c) & ((xy == 0) | (slot == 1))
    mine = exact(picks(hit), weight_ref[...].reshape(27 * 64, 128))
    o, k = grid_of((128, 256))
    spread = [exact(mine, picks((((k >> 3) & 1) == s) & (o == (k >> 4) * 8 + (k & 7)))) for s in range(2)]
    for_own = jnp.concatenate([spread[0][48:], spread[1][48:]], axis=0)
    for_next = jnp.concatenate([spread[0][:48], spread[1][:48]], axis=0)
    return for_own, for_next


def plane_of(ref):
    return jnp.concatenate([ref[:, hh].reshape(256, COLS) for hh in range(16)], axis=1)


def views_of(ref):
    return jnp.concatenate([ref[hh].reshape(256, COLS) for hh in range(16)], axis=1)


def kernel_terms(own_ref, views_ref):
    both = lax.dot_general(
        plane_of(own_ref), views_of(views_ref), (((1,), (1,)), ((), ())), preferred_element_type=F32
    ).reshape(16, 16, 256)
    return both[:, :8, :128] + both[:, 8:, 128:]


def input_terms(own_ref, next_ref, for_own, for_next):
    from_own = mm(for_own, plane_of(own_ref))
    from_next = mm(for_next, plane_of(next_ref))
    nothing = jnp.zeros((8, COLS), F32)
    w = lax.broadcasted_iota(jnp.int32, (8, 2048), 1) & 127

    def tap(product, tiles, tile, s):
        at = 16 * (s * tiles + tile)
        above = product[at + 8 : at + 16, COLS:]
        if s == 0:
            crossing = product[16 * tiles + 16 * tile + 8 : 16 * tiles + 16 * tile + 16, :COLS]
        else:
            crossing = nothing
        return product[at : at + 8] + jnp.concatenate([above, crossing], axis=1)

    r, k = grid_of((256, 256))
    lanes = picks(k == 2 * (r & 127) + (r >> 7))
    rows = picks(((r >> 6) == (k & 3)) & ((r & 63) == 2 * (k >> 3) + ((k >> 2) & 1)))
    planes = []
    for p in range(2):
        halves = []
        for s in range(2):
            by_e = [tap(from_own, 6, 3 * p + e, s) for e in range(3)]
            if p == 1:
                by_e = [by_e[e] + tap(from_next, 3, e, s) for e in range(3)]
            shifted = jnp.where(w == 127, 0.0, pltpu.roll(by_e[0], 2047, 1))
            even, odd = by_e[1], by_e[2] + shifted
            halves.append(
                jnp.concatenate(
                    [
                        jnp.concatenate([v[:, COLS * hh : COLS * hh + COLS] for hh in range(16)], axis=0)
                        for v in (even, odd)
                    ],
                    axis=1,
                )
            )
        mixed = jnp.concatenate(halves, axis=0).astype(BF16)
        planes.append(exact(rows, exact(mixed, lanes)).reshape(CI, 64, 256))
    return planes


def body(
    grad_hbm, volume_hbm, weight_hbm, result, kernel_ref,
    own, nxt, views, grad, volume, halo, weight, parts, arrived,
    recv_own, recv_next, recv_halo, recv_parts,
    send_plane, send_chip, send_halo, send_parts, local, know,
):
    depth, chan = lax.axis_index("depth"), lax.axis_index("chan")
    core, zh, y = depth % 2, (depth // 2) % 4, depth // 8
    x, zl = chan % NX, chan // NX
    z = zh * NZL + zl

    def at(x_, y_, z_, core_):
        return ((y_ * 4 + z_ // NZL) * 2 + core_, (z_ % NZL) * NX + x_)

    xr, xl, x2 = (x + 1) % NX, (x + 3) % NX, (x + 2) % NX
    right, left = (depth, zl * NX + xr), (depth, zl * NX + xl)
    partner = (depth + 1 - 2 * core, chan)
    far = (depth, zl * NX + x2)
    row = (zl, zl + 1 - 2 * (zl % 2), (zl + 2) % NZL, NZL - 1 - zl)
    column = tuple((depth, v * NX + x) for v in row)
    here = tuple(v * NX + x for v in row)
    others = tuple(tuple(v * NX + c for c in (xl, xr, x2)) for v in row)

    far = (depth, zl * NX + x2)
    row = (zl, zl + 1 - 2 * (zl % 2), (zl + 2) % NZL, NZL - 1 - zl)
    column = tuple((depth, v * NX + x) for v in row)
    here = tuple(v * NX + x for v in row)
    others = tuple(tuple(v * NX + c for c in (xl, xr, x2)) for v in row)

    def up(n):
        return at(x, y, (z + n) % NZ, core), at(x, y, (z + NZ - n) % NZ, core)

    beside = (at(x, (y + 1) % NY, z, core), at(x, (y + 3) % NY, z, core))

    barrier = pltpu.get_barrier_semaphore()

    def greet(device, sem=barrier):
        pl.semaphore_signal(sem, inc=1, device_id=device, device_id_type=MESH)

    def when(condition, act, *args):
        pl.when(condition)(lambda: act(*args))

    for device in (far, right, left, *column[1:], partner):
        greet(device)
    take_grad = pltpu.make_async_copy(grad_hbm, grad, local.at[3])
    take_grad.start()
    above, below = ((depth + 1) % DEPTH, chan), ((depth + DEPTH - 1) % DEPTH, chan)
    has_above, has_below = depth < DEPTH - 1, depth > 0

    calls_above, calls_below = (core == 1) & (zh < 3), (core == 0) & (zh == 0) & has_below
    heard_below, heard_above = (core == 0) & (zh > 0), (core == 1) & (zh == 3) & has_above

    def plane_mates(ys):
        return [((y_ * 4 + zh) * 2 + core_, chan) for y_ in ys for core_ in range(2)]

    def across_groups(zh_):
        return at(x, y, zh_ * NZL + zl, core)

    def greet_all(devices, sem=barrier):
        for device in devices:
            greet(device, sem)

    for y_, later in ((0, (1, 3, 2)), (1, (3, 2)), (3, (2,))):
        when(y == y_, greet_all, plane_mates(later))
    when(calls_above, greet, above)
    when(calls_below, greet, below)
    when(zh == 0, greet_all, [across_groups(1), across_groups(3)])
    when(zh == 1, greet, across_groups(2))
    y_rank = jnp.where(y == 2, 3, jnp.where(y == 3, 2, y))
    take_volume = pltpu.make_async_copy(volume_hbm, volume, local.at[0])
    take_weight = pltpu.make_async_copy(weight_hbm, weight, local.at[1])
    take_volume.start()
    take_weight.start()
    take_grad.wait()
    own[chan] = packed_shard(grad[...].reshape(8, ROWS, COLS))
    greeted = 7 + 2 * y_rank + jnp.minimum(zh, 1) + jnp.where(heard_below | heard_above, 1, 0)
    pl.semaphore_wait(barrier, greeted)

    class Plane:
        def __init__(self, ref, recv, sem, each):
            self.ref, self.recv, self.sem, self.each = ref, recv, sem, each

        def copy(self, slot, device):
            return pltpu.make_async_remote_copy(
                self.ref.at[slot], self.ref.at[slot], self.sem, self.recv.at[slot],
                device_id=device, device_id_type=MESH,
            )

        def sides(self, slot):
            for device in (far, right, left):
                self.copy(slot, device).start()

        def begin(self):
            self.sides(chan)
            for k in (1, 3, 2):
                self.copy(chan, column[k]).start()
            self.each(chan)

        def wait(self, slot):
            self.copy(slot, partner).wait_recv()
            self.each(slot)

        def column_of(self, k):
            self.copy(here[k], partner).wait_recv()
            self.sides(here[k])
            self.each(here[k])

        def rest_of(self, k):
            for slot in others[k]:
                self.wait(slot)

        def sent(self):
            shards_ = self.ref.at[pl.ds(0, CHAN - 1)]
            pltpu.make_async_remote_copy(
                shards_, shards_, self.sem, self.recv.at[0], device_id=partner, device_id_type=MESH
            ).wait_send()

    def to_partner(slot):
        return pltpu.make_async_remote_copy(
            own.at[slot], nxt.at[slot], send_chip, recv_next.at[slot],
            device_id=partner, device_id_type=MESH,
        )

    def hand(slot):
        when(core == 1, lambda: to_partner(slot).start())

    mine = Plane(own, recv_own, send_plane.at[0], hand)
    after = Plane(nxt, recv_next, send_plane.at[1], lambda slot: None)

    def plane_up():
        return pltpu.make_async_remote_copy(
            volume_hbm.at[:, 1], halo, send_halo.at[0], recv_halo,
            device_id=((depth + 1) % DEPTH, chan), device_id_type=MESH,
        )

    def shard_down():
        return pltpu.make_async_remote_copy(
            own.at[chan], nxt.at[chan], send_halo.at[1], recv_next.at[chan],
            device_id=((depth + DEPTH - 1) % DEPTH, chan), device_id_type=MESH,
        )

    def trade_down():
        pl.semaphore_wait(know.at[1], 1)
        shard_down().start()

    def trade_up():
        pl.semaphore_wait(know.at[1], 1)
        plane_up().start()

    def next_rows():
        shard_down().wait_recv()
        after.begin()
        for k in (1, 3, 2):
            after.column_of(k)

    def tell(zh_, n):
        greet(across_groups(zh_), know.at[n])

    def hear(*semaphores):
        for n in semaphores:
            pl.semaphore_wait(know.at[n], 1)

    def whole_plane():
        when(y != 2, lambda: pl.semaphore_wait(know.at[0], 2 * (3 - y_rank)))
        for zh_, earlier in ((1, 0), (2, 1), (3, 0)):
            when(zh == zh_, tell, earlier, 2 + zh_)

    def first_news():
        @pl.when(zh == 0)
        def _():
            hear(3, 5)
            tell(1, 2)

        @pl.when(zh == 1)
        def _():
            hear(4)
            tell(0, 4)

    def last_news():
        @pl.when(zh == 0)
        def _():
            hear(4)
            tell(3, 2)

        @pl.when(zh == 1)
        def _():
            hear(2)
            tell(2, 2)

    def trade():
        when(heard_above, lambda: plane_up().start())
        when(calls_above, trade_up)

    late, early = zh > 0, zh == 0
    gathers_next = (core == 1) & has_above
    mine.begin()
    when(core == 0, lambda: plane_up().start())
    when(heard_below & (zh == 1), lambda: shard_down().start())
    when(heard_below, greet, below, know.at[1])
    when(heard_above, greet, above, know.at[1])
    for y_, sooner in ((1, (0,)), (3, (0, 1)), (2, (0, 1, 3))):
        when(y == y_, greet_all, plane_mates(sooner), know.at[0])
    whole_plane()
    mine.column_of(1)
    mine.rest_of(0)
    mine.column_of(3)
    mine.column_of(2)
    when(late, trade)
    when(heard_below & (zh > 1), lambda: shard_down().start())
    take_volume.wait()
    own_views(volume, views)
    when(early, trade)
    when(calls_below, trade_down)
    first_news()
    mine.rest_of(1)
    last_news()
    when(has_below, lambda: plane_up().wait_recv())

    @pl.when(depth == 0)
    def _():
        halo[...] = jnp.zeros_like(halo)

    halo_views(halo, views)
    when(gathers_next & early, next_rows)
    mine.rest_of(2)
    mine.rest_of(3)
    terms = kernel_terms(own, views)
    parts[:, 0] = terms[:, :4]
    parts[:, 1] = terms[:, 4:]
    when(zh > 1, hear, 2)
    for step in FAR_FIRST:
        dy, dz, dc = step // 8, (step // 2) % 4, step % 2
        peer = (((y + dy) % NY) * 4 + (zh + dz) % 4) * 2 + (core + dc) % 2
        pltpu.make_async_remote_copy(
            parts.at[peer // 2, peer % 2], arrived.at[step - 1], send_parts, recv_parts,
            device_id=(peer, chan), device_id_type=MESH,
        ).start()

    take_weight.wait()
    for_own, for_next = own_weights(weight, chan)
    when(gathers_next & late, next_rows)

    @pl.when(gathers_next)
    def _():
        for k in range(4):
            after.rest_of(k)

    @pl.when(depth == DEPTH - 1)
    def _():
        nxt[...] = jnp.zeros_like(nxt)

    @pl.when(core == 0)
    def _():
        for slot in range(CHAN):
            to_partner(slot).wait_recv()

    planes = input_terms(own, nxt, for_own, for_next)
    for p in range(2):
        result[:, p] = planes[p]
    choose = column_order()
    every_part = pltpu.make_async_remote_copy(
        arrived, arrived, send_parts, recv_parts, device_id=partner, device_id_type=MESH
    )
    every_part.wait_recv()
    total = parts[depth // 2, depth % 2] + jnp.sum(arrived[...], axis=0)
    chosen = jnp.dot(
        jnp.concatenate([total, total], axis=0), choose, precision=lax.Precision.HIGHEST, preferred_element_type=F32
    )
    chosen = chosen * (1.0 / math.sqrt(DEPTH * ROWS * COLS))
    for c in range(CI):
        kernel_ref[c] = chosen[:4, 32 * c : 32 * c + 27]
    mine.sent()
    when(gathers_next, after.sent)

    @pl.when(core == 1)
    def _():
        pltpu.make_async_remote_copy(
            own, nxt, send_chip, recv_next.at[0], device_id=partner, device_id_type=MESH
        ).wait_send()

    when(depth < DEPTH - 1, lambda: plane_up().wait_send())
    when((core == 0) & (depth > 0), lambda: shard_down().wait_send())
    every_part.wait_send()


def shards(grad_out, volume, weight):
    any_space = pl.BlockSpec(memory_space=pl.ANY)
    in_vmem = pl.BlockSpec(memory_space=pltpu.VMEM)
    dma = pltpu.SemaphoreType.DMA
    plane = pltpu.VMEM((CHAN, 16, 16, COLS), BF16)
    input_grad, kernel_grad = pl.pallas_call(
        body,
        out_shape=(pltpu.VMEM(volume.shape, BF16), pltpu.VMEM((CI, 4, 27), F32)),
        in_specs=[any_space, any_space, any_space],
        out_specs=(in_vmem, in_vmem),
        scratch_shapes=[
            plane,
            plane,
            pltpu.VMEM((16, 2, 8, 16, COLS), BF16),
            pltpu.VMEM(grad_out.shape, BF16),
            pltpu.VMEM(volume.shape, BF16),
            pltpu.VMEM((CI, 64, 256), BF16),
            pltpu.VMEM(weight.shape, BF16),
            pltpu.VMEM((16, 2, 4, 128), F32),
            pltpu.VMEM((DEPTH - 1, 4, 128), F32),
            dma((CHAN,)),
            dma((CHAN,)),
            dma,
            dma,
            dma((2,)),
            dma,
            dma((2,)),
            dma,
            dma((4,)),
            pltpu.SemaphoreType.REGULAR((6,)),
        ],
        compiler_params=pltpu.CompilerParams(collective_id=0, has_side_effects=True),
    )(grad_out, volume, weight)
    return input_grad, jnp.transpose(kernel_grad, (2, 0, 1))


def solution(mesh):
    in_specs = (P("chan", "depth", None, None), P("chan", "depth", None, None), P())
    out_specs = (P("chan", "depth", None, None), P(None, "chan", "depth"))
    return jax.shard_map(shards, mesh=mesh, in_specs=in_specs, out_specs=out_specs, check_vma=False)
```

```python
import math

import jax
import jax.numpy as jnp
from jax import lax
from jax.experimental import pallas as pl
from jax.experimental.pallas import tpu as pltpu
from jax.sharding import PartitionSpec as P

MESH = pl.DeviceIdType.MESH
BF16 = jnp.bfloat16
F32 = jnp.float32
NX, NY, NZ, NZL, DEPTH, CHAN = 4, 4, 16, 4, 32, 16
CI, ROWS, COLS = 4, 32, 128
CUT = 8
FAR_FIRST = sorted(range(1, 32), key=lambda n: -(4 * min(n // 2 % 4, 4 - n // 2 % 4) + min(n // 8, 4 - n // 8)))


def grid_of(shape):
    return lax.broadcasted_iota(jnp.int32, shape, 0), lax.broadcasted_iota(jnp.int32, shape, 1)


def picks(mask):
    return jnp.where(mask, 1.0, 0.0).astype(BF16)


def mm(a, b):
    return jnp.dot(a, b, preferred_element_type=F32)


def exact(a, b):
    return mm(a, b).astype(BF16)


def packed_shard(block):
    r, k = grid_of((256, 256))
    rows = picks(k == (r & 7) * 32 + ((r >> 3) & 1) * 16 + (r >> 4))
    return exact(rows, block.reshape(256, COLS)).reshape(16, 16, COLS)


def column_views(plane):
    l, k = grid_of((256, 384))
    return exact(plane.reshape(256, 256), picks(l == 2 * (k & 127) + (k >> 7) - 1))


def row_picker(offset_of, keep):
    row, k = grid_of((512, 256))
    h, r = row >> 4, row & 15
    hit = ((k >> 6) == (r & 3)) & ((k & 63) == 2 * h + offset_of(r)) & keep(r)
    return picks(hit)


def own_views(volume_ref, views_ref):
    picker = row_picker(lambda r: (r >> 2) - 1, lambda r: r < 12)
    for p in range(2):
        taken = exact(picker, column_views(volume_ref[:, p]))
        for s in range(2):
            for e in range(3):
                part = taken[256 * s : 256 * s + 256, 128 * e : 128 * e + 128]
                views_ref[:, s, 3 * p + e] = part.reshape(16, 16, COLS)


def halo_views(halo_ref, views_ref):
    columns = column_views(halo_ref[...])
    for b in range(2):
        taken = exact(row_picker(lambda r, b=b: b - 1, lambda r: r >= 12), columns)
        for s in range(2):
            for e in range(3):
                part = taken[256 * s : 256 * s + 256, 128 * e : 128 * e + 128]
                views_ref[:, s, 3 * b + e] += part.reshape(16, 16, COLS)
    last = jnp.zeros((512, COLS), F32)
    for e in range(3):
        picker = row_picker(lambda r: 1, lambda r, e=e: (r >> 2) == e)
        last = last + mm(picker, columns[:, 128 * e : 128 * e + 128])
    last = last.astype(BF16)
    for s in range(2):
        views_ref[:, s, 6] = last[256 * s : 256 * s + 256].reshape(16, 16, COLS)
        views_ref[:, s, 7] = jnp.zeros((16, 16, COLS), BF16)


def column_order():
    col, k = grid_of((128, 128))
    c, t = k >> 5, k & 31
    a, b, e = t // 9, (t // 3) % 3, t % 3
    source = jnp.where(a > 0, 16 * (3 * a - 3 + e) + 4 * b, jnp.where(b < 2, 16 * (3 * b + e) + 12, 96 + 4 * e))
    return jnp.where((col == source + c) & (t < 27), 1.0, 0.0)


def own_weights(weight_ref, chan):
    m, k = grid_of((144, 27 * 64))
    a, rest = m // 48, m % 48
    e, xy, slot, c = rest >> 4, (rest >> 3) & 1, (rest >> 2) & 1, rest & 3
    b = jnp.where(xy == 0, 1 + slot, 0)
    hit = (k == (9 * a + 3 * b + e) * 64 + CI * chan + c) & ((xy == 0) | (slot == 1))
    mine = exact(picks(hit), weight_ref[...].reshape(27 * 64, 128))
    o, k = grid_of((128, 256))
    spread = [exact(mine, picks((((k >> 3) & 1) == s) & (o == (k >> 4) * 8 + (k & 7)))) for s in range(2)]
    for_own = jnp.concatenate([spread[0][48:], spread[1][48:]], axis=0)
    for_next = jnp.concatenate([spread[0][:48], spread[1][:48]], axis=0)
    return for_own, for_next


def plane_of(ref):
    return jnp.concatenate([ref[:, hh].reshape(256, COLS) for hh in range(16)], axis=1)


def views_of(ref):
    return jnp.concatenate([ref[hh].reshape(256, COLS) for hh in range(16)], axis=1)


def kernel_terms(own_ref, views_ref):
    both = lax.dot_general(
        plane_of(own_ref), views_of(views_ref), (((1,), (1,)), ((), ())), preferred_element_type=F32
    ).reshape(16, 16, 256)
    return both[:, :8, :128] + both[:, 8:, 128:]


def input_terms(own_ref, next_ref, for_own, for_next):
    from_own = mm(for_own, plane_of(own_ref))
    from_next = mm(for_next, plane_of(next_ref))
    nothing = jnp.zeros((8, COLS), F32)
    w = lax.broadcasted_iota(jnp.int32, (8, 2048), 1) & 127

    def tap(product, tiles, tile, s):
        at = 16 * (s * tiles + tile)
        above = product[at + 8 : at + 16, COLS:]
        if s == 0:
            crossing = product[16 * tiles + 16 * tile + 8 : 16 * tiles + 16 * tile + 16, :COLS]
        else:
            crossing = nothing
        return product[at : at + 8] + jnp.concatenate([above, crossing], axis=1)

    r, k = grid_of((256, 256))
    lanes = picks(k == 2 * (r & 127) + (r >> 7))
    rows = picks(((r >> 6) == (k & 3)) & ((r & 63) == 2 * (k >> 3) + ((k >> 2) & 1)))
    planes = []
    for p in range(2):
        halves = []
        for s in range(2):
            by_e = [tap(from_own, 6, 3 * p + e, s) for e in range(3)]
            if p == 1:
                by_e = [by_e[e] + tap(from_next, 3, e, s) for e in range(3)]
            shifted = jnp.where(w == 127, 0.0, pltpu.roll(by_e[0], 2047, 1))
            even, odd = by_e[1], by_e[2] + shifted
            halves.append(
                jnp.concatenate(
                    [
                        jnp.concatenate([v[:, COLS * hh : COLS * hh + COLS] for hh in range(16)], axis=0)
                        for v in (even, odd)
                    ],
                    axis=1,
                )
            )
        mixed = jnp.concatenate(halves, axis=0).astype(BF16)
        planes.append(exact(rows, exact(mixed, lanes)).reshape(CI, 64, 256))
    return planes


def body(
    grad_hbm, volume_hbm, weight_hbm, result, kernel_ref,
    own, nxt, views, grad, volume, halo, weight, parts, arrived,
    recv_own, recv_next, recv_halo, recv_parts,
    send_plane, send_chip, send_halo, send_parts, local, know,
):
    depth, chan = lax.axis_index("depth"), lax.axis_index("chan")
    core, zh, y = depth % 2, (depth // 2) % 4, depth // 8
    x, zl = chan % NX, chan // NX
    z = zh * NZL + zl

    def at(x_, y_, z_, core_):
        return ((y_ * 4 + z_ // NZL) * 2 + core_, (z_ % NZL) * NX + x_)

    xr, xl, x2 = (x + 1) % NX, (x + 3) % NX, (x + 2) % NX
    right, left = (depth, zl * NX + xr), (depth, zl * NX + xl)
    partner = (depth + 1 - 2 * core, chan)
    far = (depth, zl * NX + x2)
    row = (zl, zl + 1 - 2 * (zl % 2), (zl + 2) % NZL, NZL - 1 - zl)
    column = tuple((depth, v * NX + x) for v in row)
    here = tuple(v * NX + x for v in row)
    others = tuple(tuple(v * NX + c for c in (xl, xr, x2)) for v in row)

    far = (depth, zl * NX + x2)
    row = (zl, zl + 1 - 2 * (zl % 2), (zl + 2) % NZL, NZL - 1 - zl)
    column = tuple((depth, v * NX + x) for v in row)
    here = tuple(v * NX + x for v in row)
    others = tuple(tuple(v * NX + c for c in (xl, xr, x2)) for v in row)

    def up(n):
        return at(x, y, (z + n) % NZ, core), at(x, y, (z + NZ - n) % NZ, core)

    beside = (at(x, (y + 1) % NY, z, core), at(x, (y + 3) % NY, z, core))

    barrier = pltpu.get_barrier_semaphore()

    def greet(device, sem=barrier):
        pl.semaphore_signal(sem, inc=1, device_id=device, device_id_type=MESH)

    def when(condition, act, *args):
        pl.when(condition)(lambda: act(*args))

    for device in (far, right, left, *column[1:], partner):
        greet(device)
    take_grad = pltpu.make_async_copy(grad_hbm, grad, local.at[3])
    take_grad.start()
    above, below = ((depth + 1) % DEPTH, chan), ((depth + DEPTH - 1) % DEPTH, chan)
    has_above, has_below = depth < DEPTH - 1, depth > 0

    calls_above, calls_below = (core == 1) & (zh < 3), (core == 0) & (zh == 0) & has_below
    heard_below, heard_above = (core == 0) & (zh > 0), (core == 1) & (zh == 3) & has_above

    def plane_mates(ys):
        return [((y_ * 4 + zh) * 2 + core_, chan) for y_ in ys for core_ in range(2)]

    def across_groups(zh_):
        return at(x, y, zh_ * NZL + zl, core)

    def greet_all(devices, sem=barrier):
        for device in devices:
            greet(device, sem)

    for y_, later in ((0, (1, 3, 2)), (1, (3, 2)), (3, (2,))):
        when(y == y_, greet_all, plane_mates(later))
    when(calls_above, greet, above)
    when(calls_below, greet, below)
    when(zh == 0, greet_all, [across_groups(1), across_groups(3)])
    when(zh == 1, greet, across_groups(2))
    y_rank = jnp.where(y == 2, 3, jnp.where(y == 3, 2, y))
    take_volume = pltpu.make_async_copy(volume_hbm, volume, local.at[0])
    take_weight = pltpu.make_async_copy(weight_hbm, weight, local.at[1])
    take_volume.start()
    take_weight.start()
    take_grad.wait()
    own[chan] = packed_shard(grad[...].reshape(8, ROWS, COLS))
    greeted = 7 + 2 * y_rank + jnp.minimum(zh, 1) + jnp.where(heard_below | heard_above, 1, 0)
    pl.semaphore_wait(barrier, greeted)

    odd = zl % 2 == 1

    class Plane:
        def __init__(self, ref, recv, sem, each):
            self.ref, self.recv, self.sem, self.each = ref, recv, sem, each

        def piece(self, slot, part):
            if part == 0:
                return self.ref.at[slot]
            return self.ref.at[slot, pl.ds(0, CUT)] if part == 1 else self.ref.at[slot, pl.ds(CUT, 16 - CUT)]

        def copy(self, slot, device, part=0):
            piece = self.piece(slot, part)
            return pltpu.make_async_remote_copy(
                piece, piece, self.sem.at[part], self.recv.at[2 * slot + part // 2],
                device_id=device, device_id_type=MESH,
            )

        def sides(self, slot, part=0):
            for device in (far, right, left):
                self.copy(slot, device, part).start()

        def begin(self):
            self.sides(chan)
            for k in (1, 3, 2):
                self.copy(chan, column[k]).start()
            self.each(chan)

        def wait(self, slot, *parts_):
            for part in parts_ or (0,):
                self.copy(slot, partner, part).wait_recv()

        def nearest(self):
            self.wait(here[1])
            self.sides(here[1], 2)
            when(odd, self.sides, here[1], 1)
            self.each(here[1])

        def own_row(self):
            for slot in others[0]:
                self.wait(slot)
                when(odd, lambda slot=slot: self.copy(slot, column[1], 1).start())
                self.each(slot)

        def column_of(self, k):
            self.wait(here[k])
            self.sides(here[k])
            self.each(here[k])

        def rest_of(self, k):
            for slot in others[k]:
                self.wait(slot, *((1, 2) if k == 1 else ()))
                self.each(slot)

        def drained(self, count, part):
            pieces = self.piece(pl.ds(0, count), part)
            pltpu.make_async_remote_copy(
                pieces, pieces, self.sem.at[part], self.recv.at[0], device_id=partner, device_id_type=MESH
            ).wait_send()

        def sent(self):
            self.drained(12, 0)
            self.drained(3, 2)
            when(odd, self.drained, 6, 1)

    def to_partner(slot):
        return pltpu.make_async_remote_copy(
            own.at[slot], nxt.at[slot], send_chip, recv_next.at[2 * slot],
            device_id=partner, device_id_type=MESH,
        )

    def hand(slot):
        when(core == 1, lambda: to_partner(slot).start())

    mine = Plane(own, recv_own, send_plane.at[0], hand)
    after = Plane(nxt, recv_next, send_plane.at[1], lambda slot: None)

    def plane_up():
        return pltpu.make_async_remote_copy(
            volume_hbm.at[:, 1], halo, send_halo.at[0], recv_halo,
            device_id=((depth + 1) % DEPTH, chan), device_id_type=MESH,
        )

    def shard_down():
        return pltpu.make_async_remote_copy(
            own.at[chan], nxt.at[chan], send_halo.at[1], recv_next.at[2 * chan],
            device_id=((depth + DEPTH - 1) % DEPTH, chan), device_id_type=MESH,
        )

    def trade_down():
        pl.semaphore_wait(know.at[1], 1)
        shard_down().start()

    def trade_up():
        pl.semaphore_wait(know.at[1], 1)
        plane_up().start()

    def next_rows():
        shard_down().wait_recv()
        after.begin()
        after.nearest()
        after.own_row()
        after.column_of(3)
        after.column_of(2)

    def tell(zh_, n):
        greet(across_groups(zh_), know.at[n])

    def hear(*semaphores):
        for n in semaphores:
            pl.semaphore_wait(know.at[n], 1)

    def whole_plane():
        when(y != 2, lambda: pl.semaphore_wait(know.at[0], 2 * (3 - y_rank)))
        for zh_, earlier in ((1, 0), (2, 1), (3, 0)):
            when(zh == zh_, tell, earlier, 2 + zh_)

    def first_news():
        @pl.when(zh == 0)
        def _():
            hear(3, 5)
            tell(1, 2)

        @pl.when(zh == 1)
        def _():
            hear(4)
            tell(0, 4)

    def last_news():
        @pl.when(zh == 0)
        def _():
            hear(4)
            tell(3, 2)

        @pl.when(zh == 1)
        def _():
            hear(2)
            tell(2, 2)

    def trade():
        when(heard_above, lambda: plane_up().start())
        when(calls_above, trade_up)

    late, early = zh > 0, zh == 0
    gathers_next = (core == 1) & has_above
    mine.begin()
    when(core == 0, lambda: plane_up().start())
    when(heard_below & (zh == 1), lambda: shard_down().start())
    when(heard_below, greet, below, know.at[1])
    when(heard_above, greet, above, know.at[1])
    for y_, sooner in ((1, (0,)), (3, (0, 1)), (2, (0, 1, 3))):
        when(y == y_, greet_all, plane_mates(sooner), know.at[0])
    whole_plane()
    mine.nearest()
    mine.own_row()
    mine.column_of(3)
    mine.column_of(2)
    when(late, trade)
    when(heard_below & (zh > 1), lambda: shard_down().start())
    take_volume.wait()
    own_views(volume, views)
    when(early, trade)
    when(calls_below, trade_down)
    first_news()
    mine.rest_of(1)
    when(gathers_next & early, next_rows)
    last_news()
    when(has_below, lambda: plane_up().wait_recv())

    @pl.when(depth == 0)
    def _():
        halo[...] = jnp.zeros_like(halo)

    halo_views(halo, views)
    mine.rest_of(2)
    mine.rest_of(3)
    terms = kernel_terms(own, views)
    parts[:, 0] = terms[:, :4]
    parts[:, 1] = terms[:, 4:]
    when(zh > 1, hear, 2)
    for step in FAR_FIRST:
        dy, dz, dc = step // 8, (step // 2) % 4, step % 2
        peer = (((y + dy) % NY) * 4 + (zh + dz) % 4) * 2 + (core + dc) % 2
        pltpu.make_async_remote_copy(
            parts.at[peer // 2, peer % 2], arrived.at[step - 1], send_parts, recv_parts,
            device_id=(peer, chan), device_id_type=MESH,
        ).start()

    take_weight.wait()
    for_own, for_next = own_weights(weight, chan)
    when(gathers_next & late, next_rows)

    @pl.when(gathers_next)
    def _():
        for k in range(1, 4):
            after.rest_of(k)

    @pl.when(depth == DEPTH - 1)
    def _():
        nxt[...] = jnp.zeros_like(nxt)

    @pl.when(core == 0)
    def _():
        for slot in range(CHAN):
            to_partner(slot).wait_recv()

    planes = input_terms(own, nxt, for_own, for_next)
    for p in range(2):
        result[:, p] = planes[p]
    choose = column_order()
    every_part = pltpu.make_async_remote_copy(
        arrived, arrived, send_parts, recv_parts, device_id=partner, device_id_type=MESH
    )
    every_part.wait_recv()
    total = parts[depth // 2, depth % 2] + jnp.sum(arrived[...], axis=0)
    chosen = jnp.dot(
        jnp.concatenate([total, total], axis=0), choose, precision=lax.Precision.HIGHEST, preferred_element_type=F32
    )
    chosen = chosen * (1.0 / math.sqrt(DEPTH * ROWS * COLS))
    for c in range(CI):
        kernel_ref[c] = chosen[:4, 32 * c : 32 * c + 27]
    mine.sent()
    when(gathers_next, after.sent)

    @pl.when(core == 1)
    def _():
        pltpu.make_async_remote_copy(
            own, nxt, send_chip, recv_next.at[0], device_id=partner, device_id_type=MESH
        ).wait_send()

    when(depth < DEPTH - 1, lambda: plane_up().wait_send())
    when((core == 0) & (depth > 0), lambda: shard_down().wait_send())
    every_part.wait_send()


def shards(grad_out, volume, weight):
    any_space = pl.BlockSpec(memory_space=pl.ANY)
    in_vmem = pl.BlockSpec(memory_space=pltpu.VMEM)
    dma = pltpu.SemaphoreType.DMA
    plane = pltpu.VMEM((CHAN, 16, 16, COLS), BF16)
    input_grad, kernel_grad = pl.pallas_call(
        body,
        out_shape=(pltpu.VMEM(volume.shape, BF16), pltpu.VMEM((CI, 4, 27), F32)),
        in_specs=[any_space, any_space, any_space],
        out_specs=(in_vmem, in_vmem),
        scratch_shapes=[
            plane,
            plane,
            pltpu.VMEM((16, 2, 8, 16, COLS), BF16),
            pltpu.VMEM(grad_out.shape, BF16),
            pltpu.VMEM(volume.shape, BF16),
            pltpu.VMEM((CI, 64, 256), BF16),
            pltpu.VMEM(weight.shape, BF16),
            pltpu.VMEM((16, 2, 4, 128), F32),
            pltpu.VMEM((DEPTH - 1, 4, 128), F32),
            dma((2 * CHAN,)),
            dma((2 * CHAN,)),
            dma,
            dma,
            dma((2, 3)),
            dma,
            dma((2,)),
            dma,
            dma((4,)),
            pltpu.SemaphoreType.REGULAR((6,)),
        ],
        compiler_params=pltpu.CompilerParams(collective_id=0, has_side_effects=True),
    )(grad_out, volume, weight)
    return input_grad, jnp.transpose(kernel_grad, (2, 0, 1))


def solution(mesh):
    in_specs = (P("chan", "depth", None, None), P("chan", "depth", None, None), P())
    out_specs = (P("chan", "depth", None, None), P(None, "chan", "depth"))
    return jax.shard_map(shards, mesh=mesh, in_specs=in_specs, out_specs=out_specs, check_vma=False)
```

```python
import math

import jax
import jax.numpy as jnp
from jax import lax
from jax.experimental import pallas as pl
from jax.experimental.pallas import tpu as pltpu
from jax.sharding import PartitionSpec as P

MESH = pl.DeviceIdType.MESH
BF16 = jnp.bfloat16
F32 = jnp.float32
NX, NY, NZ, NZL, DEPTH, CHAN = 4, 4, 16, 4, 32, 16
CI, ROWS, COLS = 4, 32, 128
CUT = 8
FAR_FIRST = sorted(range(1, 32), key=lambda n: -(4 * min(n // 2 % 4, 4 - n // 2 % 4) + min(n // 8, 4 - n // 8)))


def grid_of(shape):
    return lax.broadcasted_iota(jnp.int32, shape, 0), lax.broadcasted_iota(jnp.int32, shape, 1)


def picks(mask):
    return jnp.where(mask, 1.0, 0.0).astype(BF16)


def mm(a, b):
    return jnp.dot(a, b, preferred_element_type=F32)


def exact(a, b):
    return mm(a, b).astype(BF16)


def packed_shard(block):
    r, k = grid_of((256, 256))
    rows = picks(k == (r & 7) * 32 + ((r >> 3) & 1) * 16 + (r >> 4))
    return exact(rows, block.reshape(256, COLS)).reshape(16, 16, COLS)


def column_views(plane):
    l, k = grid_of((256, 384))
    return exact(plane.reshape(256, 256), picks(l == 2 * (k & 127) + (k >> 7) - 1))


def row_picker(offset_of, keep):
    row, k = grid_of((512, 256))
    h, r = row >> 4, row & 15
    hit = ((k >> 6) == (r & 3)) & ((k & 63) == 2 * h + offset_of(r)) & keep(r)
    return picks(hit)


def own_views(volume_ref, views_ref):
    picker = row_picker(lambda r: (r >> 2) - 1, lambda r: r < 12)
    for p in range(2):
        taken = exact(picker, column_views(volume_ref[:, p]))
        for s in range(2):
            for e in range(3):
                part = taken[256 * s : 256 * s + 256, 128 * e : 128 * e + 128]
                views_ref[:, s, 3 * p + e] = part.reshape(16, 16, COLS)


def halo_views(halo_ref, views_ref):
    columns = column_views(halo_ref[...])
    for b in range(2):
        taken = exact(row_picker(lambda r, b=b: b - 1, lambda r: r >= 12), columns)
        for s in range(2):
            for e in range(3):
                part = taken[256 * s : 256 * s + 256, 128 * e : 128 * e + 128]
                views_ref[:, s, 3 * b + e] += part.reshape(16, 16, COLS)
    last = jnp.zeros((512, COLS), F32)
    for e in range(3):
        picker = row_picker(lambda r: 1, lambda r, e=e: (r >> 2) == e)
        last = last + mm(picker, columns[:, 128 * e : 128 * e + 128])
    last = last.astype(BF16)
    for s in range(2):
        views_ref[:, s, 6] = last[256 * s : 256 * s + 256].reshape(16, 16, COLS)
        views_ref[:, s, 7] = jnp.zeros((16, 16, COLS), BF16)


def column_order():
    col, k = grid_of((128, 128))
    c, t = k >> 5, k & 31
    a, b, e = t // 9, (t // 3) % 3, t % 3
    source = jnp.where(a > 0, 16 * (3 * a - 3 + e) + 4 * b, jnp.where(b < 2, 16 * (3 * b + e) + 12, 96 + 4 * e))
    return jnp.where((col == source + c) & (t < 27), 1.0, 0.0)


def own_weights(weight_ref, chan):
    m, k = grid_of((144, 27 * 64))
    a, rest = m // 48, m % 48
    e, xy, slot, c = rest >> 4, (rest >> 3) & 1, (rest >> 2) & 1, rest & 3
    b = jnp.where(xy == 0, 1 + slot, 0)
    hit = (k == (9 * a + 3 * b + e) * 64 + CI * chan + c) & ((xy == 0) | (slot == 1))
    mine = exact(picks(hit), weight_ref[...].reshape(27 * 64, 128))
    o, k = grid_of((128, 256))
    spread = [exact(mine, picks((((k >> 3) & 1) == s) & (o == (k >> 4) * 8 + (k & 7)))) for s in range(2)]
    for_own = jnp.concatenate([spread[0][48:], spread[1][48:]], axis=0)
    for_next = jnp.concatenate([spread[0][:48], spread[1][:48]], axis=0)
    return for_own, for_next


def plane_of(ref):
    return jnp.concatenate([ref[:, hh].reshape(256, COLS) for hh in range(16)], axis=1)


def views_of(ref):
    return jnp.concatenate([ref[hh].reshape(256, COLS) for hh in range(16)], axis=1)


def kernel_terms(own_ref, views_ref):
    both = lax.dot_general(
        plane_of(own_ref), views_of(views_ref), (((1,), (1,)), ((), ())), preferred_element_type=F32
    ).reshape(16, 16, 256)
    return both[:, :8, :128] + both[:, 8:, 128:]


def input_terms(own_ref, next_ref, for_own, for_next):
    from_own = mm(for_own, plane_of(own_ref))
    from_next = mm(for_next, plane_of(next_ref))
    nothing = jnp.zeros((8, COLS), F32)
    w = lax.broadcasted_iota(jnp.int32, (8, 2048), 1) & 127

    def tap(product, tiles, tile, s):
        at = 16 * (s * tiles + tile)
        above = product[at + 8 : at + 16, COLS:]
        if s == 0:
            crossing = product[16 * tiles + 16 * tile + 8 : 16 * tiles + 16 * tile + 16, :COLS]
        else:
            crossing = nothing
        return product[at : at + 8] + jnp.concatenate([above, crossing], axis=1)

    r, k = grid_of((256, 256))
    lanes = picks(k == 2 * (r & 127) + (r >> 7))
    rows = picks(((r >> 6) == (k & 3)) & ((r & 63) == 2 * (k >> 3) + ((k >> 2) & 1)))
    planes = []
    for p in range(2):
        halves = []
        for s in range(2):
            by_e = [tap(from_own, 6, 3 * p + e, s) for e in range(3)]
            if p == 1:
                by_e = [by_e[e] + tap(from_next, 3, e, s) for e in range(3)]
            shifted = jnp.where(w == 127, 0.0, pltpu.roll(by_e[0], 2047, 1))
            even, odd = by_e[1], by_e[2] + shifted
            halves.append(
                jnp.concatenate(
                    [
                        jnp.concatenate([v[:, COLS * hh : COLS * hh + COLS] for hh in range(16)], axis=0)
                        for v in (even, odd)
                    ],
                    axis=1,
                )
            )
        mixed = jnp.concatenate(halves, axis=0).astype(BF16)
        planes.append(exact(rows, exact(mixed, lanes)).reshape(CI, 64, 256))
    return planes


def body(
    grad_hbm, volume_hbm, weight_hbm, result, kernel_ref,
    own, nxt, views, grad, volume, halo, weight, parts, arrived,
    recv_own, recv_next, recv_halo, recv_parts,
    send_plane, send_chip, send_halo, send_parts, local, know,
):
    depth, chan = lax.axis_index("depth"), lax.axis_index("chan")
    core, zh, y = depth % 2, (depth // 2) % 4, depth // 8
    x, zl = chan % NX, chan // NX
    z = zh * NZL + zl

    def at(x_, y_, z_, core_):
        return ((y_ * 4 + z_ // NZL) * 2 + core_, (z_ % NZL) * NX + x_)

    xr, xl, x2 = (x + 1) % NX, (x + 3) % NX, (x + 2) % NX
    right, left = (depth, zl * NX + xr), (depth, zl * NX + xl)
    partner = (depth + 1 - 2 * core, chan)
    far = (depth, zl * NX + x2)
    row = (zl, zl + 1 - 2 * (zl % 2), (zl + 2) % NZL, NZL - 1 - zl)
    column = tuple((depth, v * NX + x) for v in row)
    here = tuple(v * NX + x for v in row)
    others = tuple(tuple(v * NX + c for c in (xl, xr, x2)) for v in row)

    far = (depth, zl * NX + x2)
    row = (zl, zl + 1 - 2 * (zl % 2), (zl + 2) % NZL, NZL - 1 - zl)
    column = tuple((depth, v * NX + x) for v in row)
    here = tuple(v * NX + x for v in row)
    others = tuple(tuple(v * NX + c for c in (xl, xr, x2)) for v in row)

    def up(n):
        return at(x, y, (z + n) % NZ, core), at(x, y, (z + NZ - n) % NZ, core)

    beside = (at(x, (y + 1) % NY, z, core), at(x, (y + 3) % NY, z, core))

    barrier = pltpu.get_barrier_semaphore()

    def greet(device, sem=barrier):
        pl.semaphore_signal(sem, inc=1, device_id=device, device_id_type=MESH)

    def when(condition, act, *args):
        pl.when(condition)(lambda: act(*args))

    for device in (far, right, left, *column[1:], partner):
        greet(device)
    take_grad = pltpu.make_async_copy(grad_hbm, grad, local.at[3])
    take_grad.start()
    above, below = ((depth + 1) % DEPTH, chan), ((depth + DEPTH - 1) % DEPTH, chan)
    has_above, has_below = depth < DEPTH - 1, depth > 0

    calls_above, calls_below = (core == 1) & (zh < 3), (core == 0) & (zh == 0) & has_below
    heard_below, heard_above = (core == 0) & (zh > 0), (core == 1) & (zh == 3) & has_above

    def plane_mates(ys):
        return [((y_ * 4 + zh) * 2 + core_, chan) for y_ in ys for core_ in range(2)]

    def across_groups(zh_):
        return at(x, y, zh_ * NZL + zl, core)

    def greet_all(devices, sem=barrier):
        for device in devices:
            greet(device, sem)

    for y_, later in ((0, (1, 3, 2)), (1, (3, 2)), (3, (2,))):
        when(y == y_, greet_all, plane_mates(later))
    when(calls_above, greet, above)
    when(calls_below, greet, below)
    when(zh == 0, greet_all, [across_groups(1), across_groups(3)])
    when(zh == 1, greet, across_groups(2))
    y_rank = jnp.where(y == 2, 3, jnp.where(y == 3, 2, y))
    take_volume = pltpu.make_async_copy(volume_hbm, volume, local.at[0])
    take_weight = pltpu.make_async_copy(weight_hbm, weight, local.at[1])
    take_volume.start()
    take_weight.start()
    take_grad.wait()
    own[chan] = packed_shard(grad[...].reshape(8, ROWS, COLS))
    greeted = 7 + 2 * y_rank + jnp.minimum(zh, 1) + jnp.where(heard_below | heard_above, 1, 0)
    pl.semaphore_wait(barrier, greeted)

    odd = zl % 2 == 1

    class Plane:
        def __init__(self, ref, recv, sem, each):
            self.ref, self.recv, self.sem, self.each = ref, recv, sem, each

        def piece(self, slot, part):
            if part == 0:
                return self.ref.at[slot]
            return self.ref.at[slot, pl.ds(0, CUT)] if part == 1 else self.ref.at[slot, pl.ds(CUT, 16 - CUT)]

        def copy(self, slot, device, part=0):
            piece = self.piece(slot, part)
            return pltpu.make_async_remote_copy(
                piece, piece, self.sem.at[part], self.recv.at[2 * slot + part // 2],
                device_id=device, device_id_type=MESH,
            )

        def sides(self, slot, part=0):
            for device in (far, right, left):
                self.copy(slot, device, part).start()

        def begin(self):
            self.sides(chan)
            for k in (1, 3, 2):
                self.copy(chan, column[k]).start()
            self.each(chan)

        def wait(self, slot, *parts_):
            for part in parts_ or (0,):
                self.copy(slot, partner, part).wait_recv()

        def nearest(self):
            self.wait(here[1])
            self.sides(here[1], 2)
            when(odd, self.sides, here[1], 1)
            self.each(here[1])

        def own_row(self):
            for slot in others[0]:
                self.wait(slot)
                when(odd, lambda slot=slot: self.copy(slot, column[1], 1).start())
                self.each(slot)

        def column_of(self, k):
            self.wait(here[k])
            self.sides(here[k])
            self.each(here[k])

        def rest_of(self, k):
            for slot in others[k]:
                self.wait(slot, *((1, 2) if k == 1 else ()))
                self.each(slot)

        def drained(self, count, part):
            pieces = self.piece(pl.ds(0, count), part)
            pltpu.make_async_remote_copy(
                pieces, pieces, self.sem.at[part], self.recv.at[0], device_id=partner, device_id_type=MESH
            ).wait_send()

        def sent(self):
            self.drained(12, 0)
            self.drained(3, 2)
            when(odd, self.drained, 6, 1)

    def to_partner(slot):
        return pltpu.make_async_remote_copy(
            own.at[slot], nxt.at[slot], send_chip, recv_next.at[2 * slot],
            device_id=partner, device_id_type=MESH,
        )

    def hand(slot):
        when(core == 1, lambda: to_partner(slot).start())

    mine = Plane(own, recv_own, send_plane.at[0], hand)
    after = Plane(nxt, recv_next, send_plane.at[1], lambda slot: None)

    def plane_up():
        return pltpu.make_async_remote_copy(
            volume_hbm.at[:, 1], halo, send_halo.at[0], recv_halo,
            device_id=((depth + 1) % DEPTH, chan), device_id_type=MESH,
        )

    def shard_down():
        return pltpu.make_async_remote_copy(
            own.at[chan], nxt.at[chan], send_halo.at[1], recv_next.at[2 * chan],
            device_id=((depth + DEPTH - 1) % DEPTH, chan), device_id_type=MESH,
        )

    def trade_down():
        pl.semaphore_wait(know.at[1], 1)
        shard_down().start()

    def trade_up():
        pl.semaphore_wait(know.at[1], 1)
        plane_up().start()

    def next_rows():
        shard_down().wait_recv()
        after.begin()
        after.nearest()
        after.own_row()
        after.column_of(3)
        after.column_of(2)

    def tell(zh_, n):
        greet(across_groups(zh_), know.at[n])

    def hear(*semaphores):
        for n in semaphores:
            pl.semaphore_wait(know.at[n], 1)

    def whole_plane():
        when(y != 2, lambda: pl.semaphore_wait(know.at[0], 2 * (3 - y_rank)))
        for zh_, earlier in ((1, 0), (2, 1), (3, 0)):
            when(zh == zh_, tell, earlier, 2 + zh_)

    def first_news():
        @pl.when(zh == 0)
        def _():
            hear(3, 5)
            tell(1, 2)

        @pl.when(zh == 1)
        def _():
            hear(4)
            tell(0, 4)

    def last_news():
        @pl.when(zh == 0)
        def _():
            hear(4)
            tell(3, 2)

        @pl.when(zh == 1)
        def _():
            hear(2)
            tell(2, 2)

    def trade():
        when(heard_above, lambda: plane_up().start())
        when(calls_above, trade_up)

    late, early = zh > 0, zh == 0
    gathers_next = (core == 1) & has_above
    mine.begin()
    when(core == 0, lambda: plane_up().start())
    when(heard_below & (zh == 1), lambda: shard_down().start())
    when(heard_below, greet, below, know.at[1])
    when(heard_above, greet, above, know.at[1])
    for y_, sooner in ((1, (0,)), (3, (0, 1)), (2, (0, 1, 3))):
        when(y == y_, greet_all, plane_mates(sooner), know.at[0])
    whole_plane()
    mine.nearest()
    mine.own_row()
    when(zh == 1, trade)
    mine.column_of(3)
    mine.column_of(2)
    when(zh > 1, trade)
    when(heard_below & (zh > 1), lambda: shard_down().start())
    take_volume.wait()
    own_views(volume, views)
    when(early, trade)
    when(calls_below, trade_down)
    first_news()
    mine.rest_of(1)
    when(gathers_next & early, next_rows)
    last_news()
    when(has_below, lambda: plane_up().wait_recv())

    @pl.when(depth == 0)
    def _():
        halo[...] = jnp.zeros_like(halo)

    halo_views(halo, views)
    mine.rest_of(2)
    mine.rest_of(3)
    terms = kernel_terms(own, views)
    parts[:, 0] = terms[:, :4]
    parts[:, 1] = terms[:, 4:]
    when(zh > 1, hear, 2)
    for step in FAR_FIRST:
        dy, dz, dc = step // 8, (step // 2) % 4, step % 2
        peer = (((y + dy) % NY) * 4 + (zh + dz) % 4) * 2 + (core + dc) % 2
        pltpu.make_async_remote_copy(
            parts.at[peer // 2, peer % 2], arrived.at[step - 1], send_parts, recv_parts,
            device_id=(peer, chan), device_id_type=MESH,
        ).start()

    take_weight.wait()
    for_own, for_next = own_weights(weight, chan)
    when(gathers_next & late, next_rows)

    @pl.when(gathers_next)
    def _():
        for k in range(1, 4):
            after.rest_of(k)

    @pl.when(depth == DEPTH - 1)
    def _():
        nxt[...] = jnp.zeros_like(nxt)

    @pl.when(core == 0)
    def _():
        for slot in range(CHAN):
            to_partner(slot).wait_recv()

    planes = input_terms(own, nxt, for_own, for_next)
    for p in range(2):
        result[:, p] = planes[p]
    choose = column_order()
    every_part = pltpu.make_async_remote_copy(
        arrived, arrived, send_parts, recv_parts, device_id=partner, device_id_type=MESH
    )
    every_part.wait_recv()
    total = parts[depth // 2, depth % 2] + jnp.sum(arrived[...], axis=0)
    chosen = jnp.dot(
        jnp.concatenate([total, total], axis=0), choose, precision=lax.Precision.HIGHEST, preferred_element_type=F32
    )
    chosen = chosen * (1.0 / math.sqrt(DEPTH * ROWS * COLS))
    for c in range(CI):
        kernel_ref[c] = chosen[:4, 32 * c : 32 * c + 27]
    mine.sent()
    when(gathers_next, after.sent)

    @pl.when(core == 1)
    def _():
        pltpu.make_async_remote_copy(
            own, nxt, send_chip, recv_next.at[0], device_id=partner, device_id_type=MESH
        ).wait_send()

    when(depth < DEPTH - 1, lambda: plane_up().wait_send())
    when((core == 0) & (depth > 0), lambda: shard_down().wait_send())
    every_part.wait_send()


def finish(result, sums, input_hbm, kernel_hbm, sems):
    puts = [
        pltpu.make_async_copy(result, input_hbm, sems.at[0]),
        pltpu.make_async_copy(sums, kernel_hbm, sems.at[1]),
    ]
    for put in puts:
        put.start()
    for put in puts:
        put.wait()


def shards(grad_out, volume, weight):
    any_space = pl.BlockSpec(memory_space=pl.ANY)
    in_vmem = pl.BlockSpec(memory_space=pltpu.VMEM)
    dma = pltpu.SemaphoreType.DMA
    plane = pltpu.VMEM((CHAN, 16, 16, COLS), BF16)
    input_grad, kernel_grad = pl.pallas_call(
        body,
        out_shape=(pltpu.VMEM(volume.shape, BF16), pltpu.VMEM((CI, 4, 27), F32)),
        in_specs=[any_space, any_space, any_space],
        out_specs=(in_vmem, in_vmem),
        scratch_shapes=[
            plane,
            plane,
            pltpu.VMEM((16, 2, 8, 16, COLS), BF16),
            pltpu.VMEM(grad_out.shape, BF16),
            pltpu.VMEM(volume.shape, BF16),
            pltpu.VMEM((CI, 64, 256), BF16),
            pltpu.VMEM(weight.shape, BF16),
            pltpu.VMEM((16, 2, 4, 128), F32),
            pltpu.VMEM((DEPTH - 1, 4, 128), F32),
            dma((2 * CHAN,)),
            dma((2 * CHAN,)),
            dma,
            dma,
            dma((2, 3)),
            dma,
            dma((2,)),
            dma,
            dma((4,)),
            pltpu.SemaphoreType.REGULAR((6,)),
        ],
        compiler_params=pltpu.CompilerParams(collective_id=0, has_side_effects=True),
    )(grad_out, volume, weight)
    input_grad, kernel_grad = pl.pallas_call(
        finish,
        out_shape=(jax.ShapeDtypeStruct(volume.shape, BF16), jax.ShapeDtypeStruct((CI, 4, 27), F32)),
        in_specs=[in_vmem, in_vmem],
        out_specs=(any_space, any_space),
        scratch_shapes=[dma((2,))],
    )(
        pltpu.with_memory_space_constraint(input_grad, pltpu.VMEM),
        pltpu.with_memory_space_constraint(kernel_grad, pltpu.VMEM),
    )
    return input_grad, jnp.transpose(kernel_grad, (2, 0, 1))


def solution(mesh):
    in_specs = (P("chan", "depth", None, None), P("chan", "depth", None, None), P())
    out_specs = (P("chan", "depth", None, None), P(None, "chan", "depth"))
    return jax.shard_map(shards, mesh=mesh, in_specs=in_specs, out_specs=out_specs, check_vma=False)
```

```python
import math

import jax
import jax.numpy as jnp
from jax import lax
from jax.experimental import pallas as pl
from jax.experimental.pallas import tpu as pltpu
from jax.sharding import PartitionSpec as P

MESH = pl.DeviceIdType.MESH
BF16 = jnp.bfloat16
F32 = jnp.float32
NX, NY, NZ, NZL, DEPTH, CHAN = 4, 4, 16, 4, 32, 16
CI, ROWS, COLS = 4, 32, 128
CUT = 8
FAR_FIRST = sorted(range(1, 32), key=lambda n: -(4 * min(n // 2 % 4, 4 - n // 2 % 4) + min(n // 8, 4 - n // 8)))


def grid_of(shape):
    return lax.broadcasted_iota(jnp.int32, shape, 0), lax.broadcasted_iota(jnp.int32, shape, 1)


def picks(mask):
    return jnp.where(mask, 1.0, 0.0).astype(BF16)


def mm(a, b):
    return jnp.dot(a, b, preferred_element_type=F32)


def exact(a, b):
    return mm(a, b).astype(BF16)


def packed_shard(block):
    r, k = grid_of((256, 256))
    rows = picks(k == (r & 7) * 32 + ((r >> 3) & 1) * 16 + (r >> 4))
    return exact(rows, block.reshape(256, COLS)).reshape(16, 16, COLS)


def column_views(plane):
    l, k = grid_of((256, 384))
    return exact(plane.reshape(256, 256), picks(l == 2 * (k & 127) + (k >> 7) - 1))


def row_picker(offset_of, keep):
    row, k = grid_of((512, 256))
    h, r = row >> 4, row & 15
    hit = ((k >> 6) == (r & 3)) & ((k & 63) == 2 * h + offset_of(r)) & keep(r)
    return picks(hit)


def own_views(volume_ref, views_ref):
    picker = row_picker(lambda r: (r >> 2) - 1, lambda r: r < 12)
    for p in range(2):
        taken = exact(picker, column_views(volume_ref[:, p]))
        for s in range(2):
            for e in range(3):
                part = taken[256 * s : 256 * s + 256, 128 * e : 128 * e + 128]
                views_ref[:, s, 3 * p + e] = part.reshape(16, 16, COLS)


def halo_views(halo_ref, views_ref):
    columns = column_views(halo_ref[...])
    for b in range(2):
        taken = exact(row_picker(lambda r, b=b: b - 1, lambda r: r >= 12), columns)
        for s in range(2):
            for e in range(3):
                part = taken[256 * s : 256 * s + 256, 128 * e : 128 * e + 128]
                views_ref[:, s, 3 * b + e] += part.reshape(16, 16, COLS)
    last = jnp.zeros((512, COLS), F32)
    for e in range(3):
        picker = row_picker(lambda r: 1, lambda r, e=e: (r >> 2) == e)
        last = last + mm(picker, columns[:, 128 * e : 128 * e + 128])
    last = last.astype(BF16)
    for s in range(2):
        views_ref[:, s, 6] = last[256 * s : 256 * s + 256].reshape(16, 16, COLS)
        views_ref[:, s, 7] = jnp.zeros((16, 16, COLS), BF16)


def column_order():
    col, k = grid_of((128, 128))
    c, t = k >> 5, k & 31
    a, b, e = t // 9, (t // 3) % 3, t % 3
    source = jnp.where(a > 0, 16 * (3 * a - 3 + e) + 4 * b, jnp.where(b < 2, 16 * (3 * b + e) + 12, 96 + 4 * e))
    return picks((col == source + c) & (t < 27))


def own_weights(weight_ref, chan):
    m, k = grid_of((144, 27 * 64))
    a, rest = m // 48, m % 48
    e, xy, slot, c = rest >> 4, (rest >> 3) & 1, (rest >> 2) & 1, rest & 3
    b = jnp.where(xy == 0, 1 + slot, 0)
    hit = (k == (9 * a + 3 * b + e) * 64 + CI * chan + c) & ((xy == 0) | (slot == 1))
    mine = exact(picks(hit), weight_ref[...].reshape(27 * 64, 128))
    o, k = grid_of((128, 256))
    spread = [exact(mine, picks((((k >> 3) & 1) == s) & (o == (k >> 4) * 8 + (k & 7)))) for s in range(2)]
    for_own = jnp.concatenate([spread[0][48:], spread[1][48:]], axis=0)
    for_next = jnp.concatenate([spread[0][:48], spread[1][:48]], axis=0)
    return for_own, for_next


def plane_of(ref):
    return jnp.concatenate([ref[:, hh].reshape(256, COLS) for hh in range(16)], axis=1)


def views_of(ref):
    return jnp.concatenate([ref[hh].reshape(256, COLS) for hh in range(16)], axis=1)


def kernel_terms(own_ref, views_ref):
    both = lax.dot_general(
        plane_of(own_ref), views_of(views_ref), (((1,), (1,)), ((), ())), preferred_element_type=F32
    ).reshape(16, 16, 256)
    return both[:, :8, :128] + both[:, 8:, 128:]


def input_terms(own_ref, next_ref, for_own, for_next):
    from_own = mm(for_own, plane_of(own_ref))
    from_next = mm(for_next, plane_of(next_ref))
    nothing = jnp.zeros((8, COLS), F32)
    w = lax.broadcasted_iota(jnp.int32, (8, 2048), 1) & 127

    def tap(product, tiles, tile, s):
        at = 16 * (s * tiles + tile)
        above = product[at + 8 : at + 16, COLS:]
        if s == 0:
            crossing = product[16 * tiles + 16 * tile + 8 : 16 * tiles + 16 * tile + 16, :COLS]
        else:
            crossing = nothing
        return product[at : at + 8] + jnp.concatenate([above, crossing], axis=1)

    r, k = grid_of((256, 256))
    lanes = picks(k == 2 * (r & 127) + (r >> 7))
    rows = picks(((r >> 6) == (k & 3)) & ((r & 63) == 2 * (k >> 3) + ((k >> 2) & 1)))
    planes = []
    for p in range(2):
        halves = []
        for s in range(2):
            by_e = [tap(from_own, 6, 3 * p + e, s) for e in range(3)]
            if p == 1:
                by_e = [by_e[e] + tap(from_next, 3, e, s) for e in range(3)]
            shifted = jnp.where(w == 127, 0.0, pltpu.roll(by_e[0], 2047, 1))
            even, odd = by_e[1], by_e[2] + shifted
            halves.append(
                jnp.concatenate(
                    [
                        jnp.concatenate([v[:, COLS * hh : COLS * hh + COLS] for hh in range(16)], axis=0)
                        for v in (even, odd)
                    ],
                    axis=1,
                )
            )
        mixed = jnp.concatenate(halves, axis=0).astype(BF16)
        planes.append(exact(rows, exact(mixed, lanes)).reshape(CI, 64, 256))
    return planes


def body(
    grad_hbm, volume_hbm, weight_hbm, result, kernel_ref,
    own, nxt, views, grad, volume, halo, weight, parts, arrived,
    recv_own, recv_next, recv_halo, recv_parts,
    send_plane, send_chip, send_halo, send_parts, local, know,
):
    depth, chan = lax.axis_index("depth"), lax.axis_index("chan")
    core, zh, y = depth % 2, (depth // 2) % 4, depth // 8
    x, zl = chan % NX, chan // NX
    z = zh * NZL + zl

    def at(x_, y_, z_, core_):
        return ((y_ * 4 + z_ // NZL) * 2 + core_, (z_ % NZL) * NX + x_)

    xr, xl, x2 = (x + 1) % NX, (x + 3) % NX, (x + 2) % NX
    right, left = (depth, zl * NX + xr), (depth, zl * NX + xl)
    partner = (depth + 1 - 2 * core, chan)
    far = (depth, zl * NX + x2)
    row = (zl, zl + 1 - 2 * (zl % 2), (zl + 2) % NZL, NZL - 1 - zl)
    column = tuple((depth, v * NX + x) for v in row)
    here = tuple(v * NX + x for v in row)
    others = tuple(tuple(v * NX + c for c in (xl, xr, x2)) for v in row)

    far = (depth, zl * NX + x2)
    row = (zl, zl + 1 - 2 * (zl % 2), (zl + 2) % NZL, NZL - 1 - zl)
    column = tuple((depth, v * NX + x) for v in row)
    here = tuple(v * NX + x for v in row)
    others = tuple(tuple(v * NX + c for c in (xl, xr, x2)) for v in row)

    def up(n):
        return at(x, y, (z + n) % NZ, core), at(x, y, (z + NZ - n) % NZ, core)

    beside = (at(x, (y + 1) % NY, z, core), at(x, (y + 3) % NY, z, core))

    barrier = pltpu.get_barrier_semaphore()

    def greet(device, sem=barrier):
        pl.semaphore_signal(sem, inc=1, device_id=device, device_id_type=MESH)

    def when(condition, act, *args):
        pl.when(condition)(lambda: act(*args))

    for device in (far, right, left, *column[1:], partner):
        greet(device)
    take_grad = pltpu.make_async_copy(grad_hbm, grad, local.at[3])
    take_grad.start()
    above, below = ((depth + 1) % DEPTH, chan), ((depth + DEPTH - 1) % DEPTH, chan)
    has_above, has_below = depth < DEPTH - 1, depth > 0

    calls_above, calls_below = (core == 1) & (zh < 3), (core == 0) & (zh == 0) & has_below
    heard_below, heard_above = (core == 0) & (zh > 0), (core == 1) & (zh == 3) & has_above

    def plane_mates(ys):
        return [((y_ * 4 + zh) * 2 + core_, chan) for y_ in ys for core_ in range(2)]

    def across_groups(zh_):
        return at(x, y, zh_ * NZL + zl, core)

    def greet_all(devices, sem=barrier):
        for device in devices:
            greet(device, sem)

    for y_, later in ((0, (1, 3, 2)), (1, (3, 2)), (3, (2,))):
        when(y == y_, greet_all, plane_mates(later))
    when(calls_above, greet, above)
    when(calls_below, greet, below)
    when(zh == 0, greet_all, [across_groups(1), across_groups(3)])
    when(zh == 1, greet, across_groups(2))
    y_rank = jnp.where(y == 2, 3, jnp.where(y == 3, 2, y))
    take_volume = pltpu.make_async_copy(volume_hbm, volume, local.at[0])
    take_weight = pltpu.make_async_copy(weight_hbm, weight, local.at[1])
    take_volume.start()
    take_weight.start()
    take_grad.wait()
    own[chan] = packed_shard(grad[...].reshape(8, ROWS, COLS))
    greeted = 7 + 2 * y_rank + jnp.minimum(zh, 1) + jnp.where(heard_below | heard_above, 1, 0)
    pl.semaphore_wait(barrier, greeted)

    odd = zl % 2 == 1

    class Plane:
        def __init__(self, ref, recv, sem, each):
            self.ref, self.recv, self.sem, self.each = ref, recv, sem, each

        def piece(self, slot, part):
            if part == 0:
                return self.ref.at[slot]
            return self.ref.at[slot, pl.ds(0, CUT)] if part == 1 else self.ref.at[slot, pl.ds(CUT, 16 - CUT)]

        def copy(self, slot, device, part=0):
            piece = self.piece(slot, part)
            return pltpu.make_async_remote_copy(
                piece, piece, self.sem.at[part], self.recv.at[2 * slot + part // 2],
                device_id=device, device_id_type=MESH,
            )

        def sides(self, slot, part=0):
            for device in (far, right, left):
                self.copy(slot, device, part).start()

        def begin(self):
            self.sides(chan)
            for k in (1, 3, 2):
                self.copy(chan, column[k]).start()
            self.each(chan)

        def wait(self, slot, *parts_):
            for part in parts_ or (0,):
                self.copy(slot, partner, part).wait_recv()

        def nearest(self):
            self.wait(here[1])
            self.sides(here[1], 2)
            when(odd, self.sides, here[1], 1)
            self.each(here[1])

        def own_row(self):
            for slot in others[0]:
                self.wait(slot)
                when(odd, lambda slot=slot: self.copy(slot, column[1], 1).start())
                self.each(slot)

        def column_of(self, k):
            self.wait(here[k])
            self.sides(here[k])
            self.each(here[k])

        def rest_of(self, k):
            for slot in others[k]:
                self.wait(slot, *((1, 2) if k == 1 else ()))
                self.each(slot)

        def drained(self, count, part):
            pieces = self.piece(pl.ds(0, count), part)
            pltpu.make_async_remote_copy(
                pieces, pieces, self.sem.at[part], self.recv.at[0], device_id=partner, device_id_type=MESH
            ).wait_send()

        def sent(self):
            self.drained(12, 0)
            self.drained(3, 2)
            when(odd, self.drained, 6, 1)

    def to_partner(slot):
        return pltpu.make_async_remote_copy(
            own.at[slot], nxt.at[slot], send_chip, recv_next.at[2 * slot],
            device_id=partner, device_id_type=MESH,
        )

    def hand(slot):
        when(core == 1, lambda: to_partner(slot).start())

    mine = Plane(own, recv_own, send_plane.at[0], hand)
    after = Plane(nxt, recv_next, send_plane.at[1], lambda slot: None)

    def plane_up():
        return pltpu.make_async_remote_copy(
            volume_hbm.at[:, 1], halo, send_halo.at[0], recv_halo,
            device_id=((depth + 1) % DEPTH, chan), device_id_type=MESH,
        )

    def shard_down():
        return pltpu.make_async_remote_copy(
            own.at[chan], nxt.at[chan], send_halo.at[1], recv_next.at[2 * chan],
            device_id=((depth + DEPTH - 1) % DEPTH, chan), device_id_type=MESH,
        )

    def trade_down():
        pl.semaphore_wait(know.at[1], 1)
        shard_down().start()

    def trade_up():
        pl.semaphore_wait(know.at[1], 1)
        plane_up().start()

    def next_rows():
        shard_down().wait_recv()
        after.begin()
        after.nearest()
        after.own_row()
        after.column_of(3)
        after.column_of(2)

    def tell(zh_, n):
        greet(across_groups(zh_), know.at[n])

    def hear(*semaphores):
        for n in semaphores:
            pl.semaphore_wait(know.at[n], 1)

    def whole_plane():
        when(y != 2, lambda: pl.semaphore_wait(know.at[0], 2 * (3 - y_rank)))
        for zh_, earlier in ((1, 0), (2, 1), (3, 0)):
            when(zh == zh_, tell, earlier, 2 + zh_)

    def first_news():
        @pl.when(zh == 0)
        def _():
            hear(3, 5)
            tell(1, 2)

        @pl.when(zh == 1)
        def _():
            hear(4)
            tell(0, 4)

    def last_news():
        @pl.when(zh == 0)
        def _():
            hear(4)
            tell(3, 2)

        @pl.when(zh == 1)
        def _():
            hear(2)
            tell(2, 2)

    def trade():
        when(heard_above, lambda: plane_up().start())
        when(calls_above, trade_up)

    late, early = zh > 0, zh == 0
    gathers_next = (core == 1) & has_above
    mine.begin()
    when(core == 0, lambda: plane_up().start())
    when(heard_below & (zh == 1), lambda: shard_down().start())
    when(heard_below, greet, below, know.at[1])
    when(heard_above, greet, above, know.at[1])
    for y_, sooner in ((1, (0,)), (3, (0, 1)), (2, (0, 1, 3))):
        when(y == y_, greet_all, plane_mates(sooner), know.at[0])
    whole_plane()
    mine.nearest()
    mine.own_row()
    when(zh == 1, trade)
    mine.column_of(3)
    mine.column_of(2)
    when(zh > 1, trade)
    when(heard_below & (zh > 1), lambda: shard_down().start())
    take_volume.wait()
    own_views(volume, views)
    when(early, trade)
    when(calls_below, trade_down)
    first_news()
    mine.rest_of(1)
    when(gathers_next & early, next_rows)
    last_news()
    when(has_below, lambda: plane_up().wait_recv())

    @pl.when(depth == 0)
    def _():
        halo[...] = jnp.zeros_like(halo)

    halo_views(halo, views)
    mine.rest_of(2)
    mine.rest_of(3)
    terms = kernel_terms(own, views)
    parts[:, 0] = terms[:, :4]
    parts[:, 1] = terms[:, 4:]
    when(zh > 1, hear, 2)
    for step in FAR_FIRST:
        dy, dz, dc = step // 8, (step // 2) % 4, step % 2
        peer = (((y + dy) % NY) * 4 + (zh + dz) % 4) * 2 + (core + dc) % 2
        pltpu.make_async_remote_copy(
            parts.at[peer // 2, peer % 2], arrived.at[step - 1], send_parts, recv_parts,
            device_id=(peer, chan), device_id_type=MESH,
        ).start()

    take_weight.wait()
    for_own, for_next = own_weights(weight, chan)
    when(gathers_next & late, next_rows)

    @pl.when(gathers_next)
    def _():
        for k in range(1, 4):
            after.rest_of(k)

    @pl.when(depth == DEPTH - 1)
    def _():
        nxt[...] = jnp.zeros_like(nxt)

    @pl.when(core == 0)
    def _():
        for slot in range(CHAN):
            to_partner(slot).wait_recv()

    planes = input_terms(own, nxt, for_own, for_next)
    for p in range(2):
        result[:, p] = planes[p]
    choose = column_order()
    every_part = pltpu.make_async_remote_copy(
        arrived, arrived, send_parts, recv_parts, device_id=partner, device_id_type=MESH
    )
    every_part.wait_recv()
    total = parts[depth // 2, depth % 2] + jnp.sum(arrived[...], axis=0)
    whole = jnp.concatenate([total, total], axis=0)
    high = whole.astype(BF16).astype(F32)
    middle = (whole - high).astype(BF16).astype(F32)
    split = jnp.concatenate([high, middle, whole - high - middle], axis=0).astype(BF16)
    chosen = mm(split, choose)
    chosen = chosen[:8] + chosen[8:16] + chosen[16:]
    chosen = chosen * (1.0 / math.sqrt(DEPTH * ROWS * COLS))
    for c in range(CI):
        kernel_ref[c] = chosen[:4, 32 * c : 32 * c + 27]
    mine.sent()
    when(gathers_next, after.sent)

    @pl.when(core == 1)
    def _():
        pltpu.make_async_remote_copy(
            own, nxt, send_chip, recv_next.at[0], device_id=partner, device_id_type=MESH
        ).wait_send()

    when(depth < DEPTH - 1, lambda: plane_up().wait_send())
    when((core == 0) & (depth > 0), lambda: shard_down().wait_send())
    every_part.wait_send()


def finish(result, sums, input_hbm, kernel_hbm, sems):
    puts = [
        pltpu.make_async_copy(result, input_hbm, sems.at[0]),
        pltpu.make_async_copy(sums, kernel_hbm, sems.at[1]),
    ]
    for put in puts:
        put.start()
    for put in puts:
        put.wait()


def shards(grad_out, volume, weight):
    any_space = pl.BlockSpec(memory_space=pl.ANY)
    in_vmem = pl.BlockSpec(memory_space=pltpu.VMEM)
    dma = pltpu.SemaphoreType.DMA
    plane = pltpu.VMEM((CHAN, 16, 16, COLS), BF16)
    input_grad, kernel_grad = pl.pallas_call(
        body,
        out_shape=(pltpu.VMEM(volume.shape, BF16), pltpu.VMEM((CI, 4, 27), F32)),
        in_specs=[any_space, any_space, any_space],
        out_specs=(in_vmem, in_vmem),
        scratch_shapes=[
            plane,
            plane,
            pltpu.VMEM((16, 2, 8, 16, COLS), BF16),
            pltpu.VMEM(grad_out.shape, BF16),
            pltpu.VMEM(volume.shape, BF16),
            pltpu.VMEM((CI, 64, 256), BF16),
            pltpu.VMEM(weight.shape, BF16),
            pltpu.VMEM((16, 2, 4, 128), F32),
            pltpu.VMEM((DEPTH - 1, 4, 128), F32),
            dma((2 * CHAN,)),
            dma((2 * CHAN,)),
            dma,
            dma,
            dma((2, 3)),
            dma,
            dma((2,)),
            dma,
            dma((4,)),
            pltpu.SemaphoreType.REGULAR((6,)),
        ],
        compiler_params=pltpu.CompilerParams(collective_id=0, has_side_effects=True),
    )(grad_out, volume, weight)
    input_grad, kernel_grad = pl.pallas_call(
        finish,
        out_shape=(jax.ShapeDtypeStruct(volume.shape, BF16), jax.ShapeDtypeStruct((CI, 4, 27), F32)),
        in_specs=[in_vmem, in_vmem],
        out_specs=(any_space, any_space),
        scratch_shapes=[dma((2,))],
    )(
        pltpu.with_memory_space_constraint(input_grad, pltpu.VMEM),
        pltpu.with_memory_space_constraint(kernel_grad, pltpu.VMEM),
    )
    return input_grad, jnp.transpose(kernel_grad, (2, 0, 1))


def solution(mesh):
    in_specs = (P("chan", "depth", None, None), P("chan", "depth", None, None), P())
    out_specs = (P("chan", "depth", None, None), P(None, "chan", "depth"))
    return jax.shard_map(shards, mesh=mesh, in_specs=in_specs, out_specs=out_specs, check_vma=False)
```

```python
import math

import jax
import jax.numpy as jnp
from jax import lax
from jax.experimental import pallas as pl
from jax.experimental.pallas import tpu as pltpu
from jax.sharding import PartitionSpec as P

MESH = pl.DeviceIdType.MESH
BF16 = jnp.bfloat16
F32 = jnp.float32
NX, NY, NZ, NZL, DEPTH, CHAN = 4, 4, 16, 4, 32, 16
CI, ROWS, COLS = 4, 32, 128
CUT = 8
FAR_FIRST = sorted(range(1, 32), key=lambda n: -(4 * min(n // 2 % 4, 4 - n // 2 % 4) + min(n // 8, 4 - n // 8)))


def grid_of(shape):
    return lax.broadcasted_iota(jnp.int32, shape, 0), lax.broadcasted_iota(jnp.int32, shape, 1)


def picks(mask):
    return jnp.where(mask, 1.0, 0.0).astype(BF16)


def mm(a, b):
    return jnp.dot(a, b, preferred_element_type=F32)


def exact(a, b):
    return mm(a, b).astype(BF16)


def packed_shard(block):
    r, k = grid_of((256, 256))
    rows = picks(k == (r & 7) * 32 + ((r >> 3) & 1) * 16 + (r >> 4))
    return exact(rows, block.reshape(256, COLS)).reshape(16, 16, COLS)


def column_views(plane):
    l, k = grid_of((256, 384))
    return exact(plane.reshape(256, 256), picks(l == 2 * (k & 127) + (k >> 7) - 1))


def row_picker(offset_of, keep):
    row, k = grid_of((512, 256))
    h, r = row >> 4, row & 15
    hit = ((k >> 6) == (r & 3)) & ((k & 63) == 2 * h + offset_of(r)) & keep(r)
    return picks(hit)


def own_views(volume_ref, views_ref):
    picker = row_picker(lambda r: (r >> 2) - 1, lambda r: r < 12)
    for p in range(2):
        taken = exact(picker, column_views(volume_ref[:, p]))
        for s in range(2):
            for e in range(3):
                part = taken[256 * s : 256 * s + 256, 128 * e : 128 * e + 128]
                views_ref[:, s, 3 * p + e] = part.reshape(16, 16, COLS)


def halo_views(halo_ref, views_ref):
    columns = column_views(halo_ref[...])
    for b in range(2):
        taken = exact(row_picker(lambda r, b=b: b - 1, lambda r: r >= 12), columns)
        for s in range(2):
            for e in range(3):
                part = taken[256 * s : 256 * s + 256, 128 * e : 128 * e + 128]
                views_ref[:, s, 3 * b + e] += part.reshape(16, 16, COLS)
    last = jnp.zeros((512, COLS), F32)
    for e in range(3):
        picker = row_picker(lambda r: 1, lambda r, e=e: (r >> 2) == e)
        last = last + mm(picker, columns[:, 128 * e : 128 * e + 128])
    last = last.astype(BF16)
    for s in range(2):
        views_ref[:, s, 6] = last[256 * s : 256 * s + 256].reshape(16, 16, COLS)
        views_ref[:, s, 7] = jnp.zeros((16, 16, COLS), BF16)


def column_order():
    col, k = grid_of((128, 128))
    c, t = k >> 5, k & 31
    a, b, e = t // 9, (t // 3) % 3, t % 3
    source = jnp.where(a > 0, 16 * (3 * a - 3 + e) + 4 * b, jnp.where(b < 2, 16 * (3 * b + e) + 12, 96 + 4 * e))
    return picks((col == source + c) & (t < 27))


def own_weights(weight_ref, chan):
    m, k = grid_of((144, 27 * 64))
    a, rest = m // 48, m % 48
    e, xy, slot, c = rest >> 4, (rest >> 3) & 1, (rest >> 2) & 1, rest & 3
    b = jnp.where(xy == 0, 1 + slot, 0)
    hit = (k == (9 * a + 3 * b + e) * 64 + CI * chan + c) & ((xy == 0) | (slot == 1))
    mine = exact(picks(hit), weight_ref[...].reshape(27 * 64, 128))
    o, k = grid_of((128, 256))
    spread = [exact(mine, picks((((k >> 3) & 1) == s) & (o == (k >> 4) * 8 + (k & 7)))) for s in range(2)]
    for_own = jnp.concatenate([spread[0][48:], spread[1][48:]], axis=0)
    for_next = jnp.concatenate([spread[0][:48], spread[1][:48]], axis=0)
    return for_own, for_next


def plane_of(ref):
    return jnp.concatenate([ref[:, hh].reshape(256, COLS) for hh in range(16)], axis=1)


def views_of(ref):
    return jnp.concatenate([ref[hh].reshape(256, COLS) for hh in range(16)], axis=1)


def kernel_terms(own_ref, views_ref):
    both = lax.dot_general(
        plane_of(own_ref), views_of(views_ref), (((1,), (1,)), ((), ())), preferred_element_type=F32
    ).reshape(16, 16, 256)
    return both[:, :8, :128] + both[:, 8:, 128:]


def input_terms(own_ref, next_ref, for_own, for_next):
    from_own = mm(for_own, plane_of(own_ref))
    from_next = mm(for_next, plane_of(next_ref))
    nothing = jnp.zeros((8, COLS), F32)
    w = lax.broadcasted_iota(jnp.int32, (8, 2048), 1) & 127

    def tap(product, tiles, tile, s):
        at = 16 * (s * tiles + tile)
        above = product[at + 8 : at + 16, COLS:]
        if s == 0:
            crossing = product[16 * tiles + 16 * tile + 8 : 16 * tiles + 16 * tile + 16, :COLS]
        else:
            crossing = nothing
        return product[at : at + 8] + jnp.concatenate([above, crossing], axis=1)

    r, k = grid_of((256, 256))
    lanes = picks(k == 2 * (r & 127) + (r >> 7))
    rows = picks(((r >> 6) == (k & 3)) & ((r & 63) == 2 * (k >> 3) + ((k >> 2) & 1)))
    planes = []
    for p in range(2):
        halves = []
        for s in range(2):
            by_e = [tap(from_own, 6, 3 * p + e, s) for e in range(3)]
            if p == 1:
                by_e = [by_e[e] + tap(from_next, 3, e, s) for e in range(3)]
            shifted = jnp.where(w == 127, 0.0, pltpu.roll(by_e[0], 2047, 1))
            even, odd = by_e[1], by_e[2] + shifted
            halves.append(
                jnp.concatenate(
                    [
                        jnp.concatenate([v[:, COLS * hh : COLS * hh + COLS] for hh in range(16)], axis=0)
                        for v in (even, odd)
                    ],
                    axis=1,
                )
            )
        mixed = jnp.concatenate(halves, axis=0).astype(BF16)
        planes.append(exact(rows, exact(mixed, lanes)).reshape(CI, 64, 256))
    return planes


def body(
    grad_hbm, volume_hbm, weight_hbm, result, kernel_ref,
    own, nxt, views, grad, volume, halo, weight, parts, arrived,
    recv_own, recv_next, recv_halo, recv_parts,
    send_plane, send_chip, send_halo, send_parts, local, know,
):
    depth, chan = lax.axis_index("depth"), lax.axis_index("chan")
    core, zh, y = depth % 2, (depth // 2) % 4, depth // 8
    x, zl = chan % NX, chan // NX
    z = zh * NZL + zl

    def at(x_, y_, z_, core_):
        return ((y_ * 4 + z_ // NZL) * 2 + core_, (z_ % NZL) * NX + x_)

    xr, xl, x2 = (x + 1) % NX, (x + 3) % NX, (x + 2) % NX
    right, left = (depth, zl * NX + xr), (depth, zl * NX + xl)
    partner = (depth + 1 - 2 * core, chan)
    far = (depth, zl * NX + x2)
    row = (zl, zl + 1 - 2 * (zl % 2), (zl + 2) % NZL, NZL - 1 - zl)
    column = tuple((depth, v * NX + x) for v in row)
    here = tuple(v * NX + x for v in row)
    others = tuple(tuple(v * NX + c for c in (xl, xr, x2)) for v in row)

    far = (depth, zl * NX + x2)
    row = (zl, zl + 1 - 2 * (zl % 2), (zl + 2) % NZL, NZL - 1 - zl)
    column = tuple((depth, v * NX + x) for v in row)
    here = tuple(v * NX + x for v in row)
    others = tuple(tuple(v * NX + c for c in (xl, xr, x2)) for v in row)

    def up(n):
        return at(x, y, (z + n) % NZ, core), at(x, y, (z + NZ - n) % NZ, core)

    beside = (at(x, (y + 1) % NY, z, core), at(x, (y + 3) % NY, z, core))

    barrier = pltpu.get_barrier_semaphore()

    def greet(device, sem=barrier):
        pl.semaphore_signal(sem, inc=1, device_id=device, device_id_type=MESH)

    def when(condition, act, *args):
        pl.when(condition)(lambda: act(*args))

    for device in (far, right, left, *column[1:], partner):
        greet(device)
    take_grad = pltpu.make_async_copy(grad_hbm, grad, local.at[3])
    take_grad.start()
    above, below = ((depth + 1) % DEPTH, chan), ((depth + DEPTH - 1) % DEPTH, chan)
    has_above, has_below = depth < DEPTH - 1, depth > 0

    calls_above, calls_below = (core == 1) & (zh < 3), (core == 0) & (zh == 0) & has_below
    heard_below, heard_above = (core == 0) & (zh > 0), (core == 1) & (zh == 3) & has_above

    def plane_mates(ys):
        return [((y_ * 4 + zh) * 2 + core_, chan) for y_ in ys for core_ in range(2)]

    def across_groups(zh_):
        return at(x, y, zh_ * NZL + zl, core)

    def greet_all(devices, sem=barrier):
        for device in devices:
            greet(device, sem)

    for y_, later in ((0, (1, 3, 2)), (1, (3, 2)), (3, (2,))):
        when(y == y_, greet_all, plane_mates(later))
    when(calls_above, greet, above)
    when(calls_below, greet, below)
    when(zh == 0, greet_all, [across_groups(1), across_groups(3)])
    when(zh == 1, greet, across_groups(2))
    y_rank = jnp.where(y == 2, 3, jnp.where(y == 3, 2, y))
    take_volume = pltpu.make_async_copy(volume_hbm, volume, local.at[0])
    take_weight = pltpu.make_async_copy(weight_hbm, weight, local.at[1])
    take_volume.start()
    take_weight.start()
    take_grad.wait()
    own[chan] = packed_shard(grad[...].reshape(8, ROWS, COLS))
    greeted = 7 + 2 * y_rank + jnp.minimum(zh, 1) + jnp.where(heard_below | heard_above, 1, 0)
    pl.semaphore_wait(barrier, greeted)

    odd = zl % 2 == 1

    class Plane:
        def __init__(self, ref, recv, sem, each):
            self.ref, self.recv, self.sem, self.each = ref, recv, sem, each

        def piece(self, slot, part):
            if part == 0:
                return self.ref.at[slot]
            return self.ref.at[slot, pl.ds(0, CUT)] if part == 1 else self.ref.at[slot, pl.ds(CUT, 16 - CUT)]

        def copy(self, slot, device, part=0):
            piece = self.piece(slot, part)
            return pltpu.make_async_remote_copy(
                piece, piece, self.sem.at[part], self.recv.at[2 * slot + part // 2],
                device_id=device, device_id_type=MESH,
            )

        def sides(self, slot, part=0):
            for device in (far, right, left):
                self.copy(slot, device, part).start()

        def begin(self):
            for k in (1, 3, 2):
                self.copy(chan, column[k]).start()
            self.sides(chan)
            self.each(chan)

        def wait(self, slot, *parts_):
            for part in parts_ or (0,):
                self.copy(slot, partner, part).wait_recv()

        def nearest(self):
            self.wait(here[1])
            self.sides(here[1], 2)
            when(odd, self.sides, here[1], 1)
            self.each(here[1])

        def own_row(self):
            for slot in others[0]:
                self.wait(slot)
                when(odd, lambda slot=slot: self.copy(slot, column[1], 1).start())
                self.each(slot)

        def column_of(self, k):
            self.wait(here[k])
            self.sides(here[k])
            self.each(here[k])

        def rest_of(self, k):
            for slot in others[k]:
                self.wait(slot, *((1, 2) if k == 1 else ()))
                self.each(slot)

        def drained(self, count, part):
            pieces = self.piece(pl.ds(0, count), part)
            pltpu.make_async_remote_copy(
                pieces, pieces, self.sem.at[part], self.recv.at[0], device_id=partner, device_id_type=MESH
            ).wait_send()

        def sent(self):
            self.drained(12, 0)
            self.drained(3, 2)
            when(odd, self.drained, 6, 1)

    def to_partner(slot):
        return pltpu.make_async_remote_copy(
            own.at[slot], nxt.at[slot], send_chip, recv_next.at[2 * slot],
            device_id=partner, device_id_type=MESH,
        )

    def hand(slot):
        when(core == 1, lambda: to_partner(slot).start())

    mine = Plane(own, recv_own, send_plane.at[0], hand)
    after = Plane(nxt, recv_next, send_plane.at[1], lambda slot: None)

    def plane_up():
        return pltpu.make_async_remote_copy(
            volume_hbm.at[:, 1], halo, send_halo.at[0], recv_halo,
            device_id=((depth + 1) % DEPTH, chan), device_id_type=MESH,
        )

    def shard_down():
        return pltpu.make_async_remote_copy(
            own.at[chan], nxt.at[chan], send_halo.at[1], recv_next.at[2 * chan],
            device_id=((depth + DEPTH - 1) % DEPTH, chan), device_id_type=MESH,
        )

    def trade_down():
        pl.semaphore_wait(know.at[1], 1)
        shard_down().start()

    def trade_up():
        pl.semaphore_wait(know.at[1], 1)
        plane_up().start()

    def next_rows():
        shard_down().wait_recv()
        after.begin()
        after.nearest()
        after.own_row()
        after.column_of(3)
        after.column_of(2)

    def tell(zh_, n):
        greet(across_groups(zh_), know.at[n])

    def hear(*semaphores):
        for n in semaphores:
            pl.semaphore_wait(know.at[n], 1)

    def whole_plane():
        when(y != 2, lambda: pl.semaphore_wait(know.at[0], 2 * (3 - y_rank)))
        for zh_, earlier in ((1, 0), (2, 1), (3, 0)):
            when(zh == zh_, tell, earlier, 2 + zh_)

    def first_news():
        @pl.when(zh == 0)
        def _():
            hear(3, 5)
            tell(1, 2)

        @pl.when(zh == 1)
        def _():
            hear(4)
            tell(0, 4)

    def last_news():
        @pl.when(zh == 0)
        def _():
            hear(4)
            tell(3, 2)

        @pl.when(zh == 1)
        def _():
            hear(2)
            tell(2, 2)

    def trade():
        when(heard_above, lambda: plane_up().start())
        when(calls_above, trade_up)

    late, early = zh > 0, zh == 0
    gathers_next = (core == 1) & has_above
    mine.begin()
    when(core == 0, lambda: plane_up().start())
    when(heard_below & (zh == 1), lambda: shard_down().start())
    when(heard_below, greet, below, know.at[1])
    when(heard_above, greet, above, know.at[1])
    for y_, sooner in ((1, (0,)), (3, (0, 1)), (2, (0, 1, 3))):
        when(y == y_, greet_all, plane_mates(sooner), know.at[0])
    whole_plane()
    mine.nearest()
    mine.own_row()
    when(zh == 1, trade)
    mine.column_of(3)
    mine.column_of(2)
    when(zh > 1, trade)
    when(heard_below & (zh > 1), lambda: shard_down().start())
    take_volume.wait()
    own_views(volume, views)
    when(early, trade)
    when(calls_below, trade_down)
    first_news()
    mine.rest_of(1)
    when(gathers_next & early, next_rows)
    last_news()
    when(has_below, lambda: plane_up().wait_recv())

    @pl.when(depth == 0)
    def _():
        halo[...] = jnp.zeros_like(halo)

    halo_views(halo, views)
    mine.rest_of(2)
    mine.rest_of(3)
    terms = kernel_terms(own, views)
    parts[:, 0] = terms[:, :4]
    parts[:, 1] = terms[:, 4:]
    when(zh > 1, hear, 2)
    for step in FAR_FIRST:
        dy, dz, dc = step // 8, (step // 2) % 4, step % 2
        peer = (((y + dy) % NY) * 4 + (zh + dz) % 4) * 2 + (core + dc) % 2
        pltpu.make_async_remote_copy(
            parts.at[peer // 2, peer % 2], arrived.at[step - 1], send_parts, recv_parts,
            device_id=(peer, chan), device_id_type=MESH,
        ).start()

    take_weight.wait()
    for_own, for_next = own_weights(weight, chan)
    when(gathers_next & late, next_rows)

    @pl.when(gathers_next)
    def _():
        for k in range(1, 4):
            after.rest_of(k)

    @pl.when(depth == DEPTH - 1)
    def _():
        nxt[...] = jnp.zeros_like(nxt)

    @pl.when(core == 0)
    def _():
        for slot in range(CHAN):
            to_partner(slot).wait_recv()

    planes = input_terms(own, nxt, for_own, for_next)
    for p in range(2):
        result[:, p] = planes[p]
    choose = column_order()
    every_part = pltpu.make_async_remote_copy(
        arrived, arrived, send_parts, recv_parts, device_id=partner, device_id_type=MESH
    )
    every_part.wait_recv()
    total = parts[depth // 2, depth % 2] + jnp.sum(arrived[...], axis=0)
    whole = jnp.concatenate([total, total], axis=0)
    high = whole.astype(BF16).astype(F32)
    middle = (whole - high).astype(BF16).astype(F32)
    split = jnp.concatenate([high, middle, whole - high - middle], axis=0).astype(BF16)
    chosen = mm(split, choose)
    chosen = chosen[:8] + chosen[8:16] + chosen[16:]
    chosen = chosen * (1.0 / math.sqrt(DEPTH * ROWS * COLS))
    for c in range(CI):
        kernel_ref[c] = chosen[:4, 32 * c : 32 * c + 27]
    mine.sent()
    when(gathers_next, after.sent)

    @pl.when(core == 1)
    def _():
        pltpu.make_async_remote_copy(
            own, nxt, send_chip, recv_next.at[0], device_id=partner, device_id_type=MESH
        ).wait_send()

    when(depth < DEPTH - 1, lambda: plane_up().wait_send())
    when((core == 0) & (depth > 0), lambda: shard_down().wait_send())
    every_part.wait_send()


def finish(result, sums, input_hbm, kernel_hbm, sems):
    puts = [
        pltpu.make_async_copy(result, input_hbm, sems.at[0]),
        pltpu.make_async_copy(sums, kernel_hbm, sems.at[1]),
    ]
    for put in puts:
        put.start()
    for put in puts:
        put.wait()


def shards(grad_out, volume, weight):
    any_space = pl.BlockSpec(memory_space=pl.ANY)
    in_vmem = pl.BlockSpec(memory_space=pltpu.VMEM)
    dma = pltpu.SemaphoreType.DMA
    plane = pltpu.VMEM((CHAN, 16, 16, COLS), BF16)
    input_grad, kernel_grad = pl.pallas_call(
        body,
        out_shape=(pltpu.VMEM(volume.shape, BF16), pltpu.VMEM((CI, 4, 27), F32)),
        in_specs=[any_space, any_space, any_space],
        out_specs=(in_vmem, in_vmem),
        scratch_shapes=[
            plane,
            plane,
            pltpu.VMEM((16, 2, 8, 16, COLS), BF16),
            pltpu.VMEM(grad_out.shape, BF16),
            pltpu.VMEM(volume.shape, BF16),
            pltpu.VMEM((CI, 64, 256), BF16),
            pltpu.VMEM(weight.shape, BF16),
            pltpu.VMEM((16, 2, 4, 128), F32),
            pltpu.VMEM((DEPTH - 1, 4, 128), F32),
            dma((2 * CHAN,)),
            dma((2 * CHAN,)),
            dma,
            dma,
            dma((2, 3)),
            dma,
            dma((2,)),
            dma,
            dma((4,)),
            pltpu.SemaphoreType.REGULAR((6,)),
        ],
        compiler_params=pltpu.CompilerParams(collective_id=0, has_side_effects=True),
    )(grad_out, volume, weight)
    input_grad, kernel_grad = pl.pallas_call(
        finish,
        out_shape=(jax.ShapeDtypeStruct(volume.shape, BF16), jax.ShapeDtypeStruct((CI, 4, 27), F32)),
        in_specs=[in_vmem, in_vmem],
        out_specs=(any_space, any_space),
        scratch_shapes=[dma((2,))],
    )(
        pltpu.with_memory_space_constraint(input_grad, pltpu.VMEM),
        pltpu.with_memory_space_constraint(kernel_grad, pltpu.VMEM),
    )
    return input_grad, jnp.transpose(kernel_grad, (2, 0, 1))


def solution(mesh):
    in_specs = (P("chan", "depth", None, None), P("chan", "depth", None, None), P())
    out_specs = (P("chan", "depth", None, None), P(None, "chan", "depth"))
    return jax.shard_map(shards, mesh=mesh, in_specs=in_specs, out_specs=out_specs, check_vma=False)
```
